128 devices in a mesh: seq: 32 (over x, y, z_lo), fsdp: 4 (over z_hi, core).
Axes of the slice: x: 4, y: 4, z: 4 (z_hi: 2, z_lo: 2; z = z_hi * 2 + z_lo), core: 2. Of those that a mesh axis runs over, the one named last changes fastest.
Arguments:
- tokens: bfloat16 [16384, 2048], P(('seq', 'fsdp')), may hold values from -6 to 6
- w_query: bfloat16 [2048, 1024], P('fsdp'), may hold values from -0.125 to 0.125
- w_key: bfloat16 [2048, 1024], P('fsdp'), may hold values from -0.125 to 0.125
- w_value: bfloat16 [2048, 2048], P('fsdp'), may hold values from -0.125 to 0.125
- w_gate_out: bfloat16 [2048, 2048], P('fsdp'), may hold values from -0.125 to 0.125
- w_beta: bfloat16 [2048, 16], P('fsdp'), may hold values from -2 to 2
- w_decay: bfloat16 [2048, 16], P('fsdp'), may hold values from -0.125 to 0.125
- conv_weight: bfloat16 [4, 4096], replicated, may hold values from -3 to 3
- decay_log: float32 [16], replicated, may hold values from -13 to -3
- dt_bias: float32 [16], replicated, may hold values from -1 to 1
- norm_gain: float32 [128], replicated, may hold values from 0.1 to 1.9
- w_out: bfloat16 [2048, 2048], P('fsdp'), may hold values from -0.125 to 0.125
Outputs:
- mixed_out: bfloat16 [16384, 2048], P(('seq', 'fsdp'))
The draws below stay inside these ranges and needn't reach their ends.
All inputs are finite; a program needn't handle non-finite values.
Results may differ from the reference program's by a relative error of at most 0.018.
Values may be sent and summed in bfloat16 or wider, within the bound.
A program may use at most 128 MiB of HBM per device.

```python
import jax
import jax.numpy as jnp
from jax import lax

D = 2048
HV = 16
DH = 128
KCONV = 4
SPAN = 128
TOKENS = 16384
QK = 1024
VW = 2048
N_FSDP = 4


def draw_tokens(key, part):
    key_first = jax.random.fold_in(key, 11)
    key_rest = jax.random.fold_in(key, 12)
    first = jax.random.uniform(key_first, (TOKENS, 1), jnp.float32, 3.0, 5.0)
    rest = jax.random.truncated_normal(key_rest, -6.0, 6.0, (TOKENS, D), jnp.float32)
    column = jnp.arange(D)[None, :] == 0
    return jnp.where(column, first, rest).astype(jnp.bfloat16)


def draw_w_beta(key, part):
    key_lead = jax.random.fold_in(key, 21)
    key_rest = jax.random.fold_in(key, 22)
    lead = jax.random.uniform(key_lead, (1, HV), jnp.float32, -8.0, -2.0) * 0.25
    rest = jax.random.truncated_normal(key_rest, -4.0, 4.0, (D, HV), jnp.float32) * 0.5 * D ** (-0.5)
    row = jnp.arange(D)[:, None] == 0
    return jnp.where(row, lead, rest).astype(jnp.bfloat16)


def draw_decay_log(key, part):
    key_pick = jax.random.fold_in(key, 31)
    key_fast = jax.random.fold_in(key, 32)
    key_slow = jax.random.fold_in(key, 33)
    order = jax.random.permutation(key_pick, HV)
    fast = order < HV // 2
    fast_rate = jax.random.uniform(key_fast, (HV,), jnp.float32, -3.5, -3.0)
    slow_rate = jax.random.uniform(key_slow, (HV,), jnp.float32, -13.0, -10.5)
    return jnp.where(fast, fast_rate, slow_rate).astype(jnp.float32)


def levels(rng, extent, shards, least, largest):
    loudness, own = 1.0, jax.random.fold_in(rng, 6)
    for axis_at, blocks in shards:
        heights = jnp.exp(jax.random.uniform(jax.random.fold_in(own, axis_at), (blocks,), jnp.float32, least / len(shards), largest / len(shards)))
        loudness = loudness * jnp.repeat(heights, extent[axis_at] // blocks).reshape([-1 if axis == axis_at else 1 for axis in range(len(extent))])
    return loudness


def gaussian(key, shape, scale, limit, shards=(), kind=jnp.bfloat16):
    array = scale * jax.random.normal(key, shape, jnp.float32)
    if shards:
        array = array * levels(key, shape, shards, -0.22, 0.18)
    return jnp.clip(array, -limit, limit).astype(kind)


def setup_inputs(seed: int = 0) -> dict:
    splits = jax.random.split(jax.random.key(seed), 13)
    tokens = draw_tokens(jax.random.fold_in(splits[12], 71), 0)
    w_query = gaussian(splits[1], (D, QK), D ** -0.5, 0.125, ((0, 4),))
    w_key = gaussian(splits[2], (D, QK), D ** -0.5, 0.125, ((0, 4),))
    w_value = gaussian(splits[3], (D, VW), D ** -0.5, 0.125, ((0, 4),))
    w_gate_out = gaussian(splits[4], (D, VW), D ** -0.5, 0.125, ((0, 4),))
    w_beta = draw_w_beta(jax.random.fold_in(splits[12], 71), 0)
    w_decay = gaussian(splits[6], (D, HV), D ** -0.5, 0.125, ((0, 4),))
    conv_weight = gaussian(splits[7], (KCONV, 2 * QK + VW), 0.5, 3.0)
    decay_log = draw_decay_log(jax.random.fold_in(splits[12], 71), 0)
    dt_bias = jnp.clip(jax.random.uniform(splits[9], (HV,), jnp.float32, -1.0, 1.0), -1.0, 1.0)
    norm_gain = jnp.clip(1.0 + 0.18 * jax.random.normal(splits[10], (DH,), jnp.float32), 0.1, 1.9)
    w_out = gaussian(splits[11], (VW, D), VW ** -0.5, 0.125, ((0, 4),))
    return {"tokens": tokens, "w_query": w_query, "w_key": w_key, "w_value": w_value, "w_gate_out": w_gate_out, "w_beta": w_beta, "w_decay": w_decay, "conv_weight": conv_weight, "decay_log": decay_log, "dt_bias": dt_bias, "norm_gain": norm_gain, "w_out": w_out}


def unit_rows(arrays):
    return arrays * lax.rsqrt(lax.optimization_barrier(jnp.sum(arrays * arrays, axis=-1, keepdims=True)) + 1e-06)

def conv_act(mixed_rows, before_rows, conv_weight):
    extended = jnp.concatenate([before_rows, mixed_rows], axis=0).astype(jnp.float32)
    count_rows = mixed_rows.shape[0]
    taps_count = conv_weight.shape[0]
    summed = conv_weight[0].astype(jnp.float32) * extended[0:count_rows]
    for offset in range(1, taps_count):
        summed = summed + conv_weight[offset].astype(jnp.float32) * extended[offset:offset + count_rows]
    return jax.nn.silu(summed).astype(jnp.bfloat16)

def head_inputs(q_cols, k_cols, v_cols, beta_cols, decay_cols, decay_log, dt_bias, head_dim):
    row_count = q_cols.shape[0]
    key_heads = q_cols.shape[1] // head_dim
    value_heads = v_cols.shape[1] // head_dim
    ratio = value_heads // key_heads
    queries = unit_rows(q_cols.astype(jnp.float32).reshape(row_count, key_heads, head_dim)) * head_dim ** (-0.5)
    key_rows = unit_rows(k_cols.astype(jnp.float32).reshape(row_count, key_heads, head_dim))
    queries = jnp.repeat(queries, ratio, axis=1)
    key_rows = jnp.repeat(key_rows, ratio, axis=1)
    values = v_cols.astype(jnp.float32).reshape(row_count, value_heads, head_dim)
    beta_gate = jax.nn.sigmoid(beta_cols.astype(jnp.float32))
    log_decay = -jnp.exp(decay_log) * jax.nn.softplus(decay_cols.astype(jnp.float32) + dt_bias)
    return (queries, key_rows, values, beta_gate, log_decay)

def span_terms(queries, key_rows, values, beta_gate, log_decay):
    highest = lax.Precision.HIGHEST
    cumul = jnp.cumsum(log_decay, axis=1)
    size_c = log_decay.shape[1]
    places = jnp.arange(size_c)
    strict = places[:, None] > places[None, :]
    within = places[:, None] >= places[None, :]
    spread = cumul[:, :, None] - cumul[:, None, :]
    fall_strict = jnp.where(strict, jnp.exp(jnp.where(strict, spread, 0.0)), 0.0)
    fall_within = jnp.where(within, jnp.exp(jnp.where(within, spread, 0.0)), 0.0)
    key_key = jnp.einsum('htd,hsd->hts', key_rows, key_rows, precision=highest)
    identity_mat = jnp.eye(size_c, dtype=jnp.float32)
    system = identity_mat + beta_gate[:, :, None] * key_key * fall_strict
    value_dim = values.shape[2]
    right_both = jnp.concatenate([beta_gate[:, :, None] * values, (beta_gate * jnp.exp(cumul))[:, :, None] * key_rows], axis=2)
    solved = jax.scipy.linalg.solve_triangular(system, right_both, lower=True)
    pseudo = solved[:, :, :value_dim]
    weights_w = solved[:, :, value_dim:]
    scores = jnp.einsum('htd,hsd->hts', queries, key_rows, precision=highest) * fall_within
    local_out = jnp.einsum('hts,hsv->htv', scores, pseudo, precision=highest)
    query_eff = jnp.exp(cumul)[:, :, None] * queries - jnp.einsum('hts,hsk->htk', scores, weights_w, precision=highest)
    tail_fall = jnp.exp(cumul[:, -1:] - cumul)
    eye_key = jnp.eye(key_rows.shape[2], dtype=jnp.float32)
    transfer = jnp.exp(cumul[:, -1])[:, None, None] * eye_key - jnp.einsum('htk,htj->hkj', weights_w * tail_fall[:, :, None], key_rows, precision=highest)
    offset_map = jnp.einsum('htv,htk->hvk', pseudo * tail_fall[:, :, None], key_rows, precision=highest)
    return (local_out, query_eff, transfer, offset_map)

def gate_norm(core_rows, gate_cols, norm_gain):
    normed = core_rows * lax.rsqrt(lax.optimization_barrier(jnp.mean(core_rows * core_rows, axis=-1, keepdims=True)) + 1e-06) * norm_gain
    gated = normed * jax.nn.silu(gate_cols.astype(jnp.float32).reshape(core_rows.shape))
    return gated.reshape(core_rows.shape[0], -1).astype(jnp.bfloat16)

def reference(tokens, w_query, w_key, w_value, w_gate_out, w_beta, w_decay, conv_weight, decay_log, dt_bias, norm_gain, w_out):
    highest = lax.Precision.HIGHEST
    block_count = TOKENS // SPAN
    tok_blocks = tokens.reshape(block_count, SPAN, D)
    out_groups = w_out.astype(jnp.float32).reshape(N_FSDP, VW // N_FSDP, D)

    def advance(carried, block_rows):
        state, rim_rows = carried
        projected = [jnp.dot(block_rows.astype(jnp.float32), weight_mat.astype(jnp.float32), preferred_element_type=jnp.float32).astype(jnp.bfloat16) for weight_mat in (w_query, w_key, w_value, w_gate_out, w_beta, w_decay)]
        mixed_rows = jnp.concatenate(projected[:3], axis=1)
        conv_out = conv_act(mixed_rows, rim_rows, conv_weight)
        queries, key_rows, values, beta_gate, log_decay = head_inputs(conv_out[:, :QK], conv_out[:, QK:2 * QK], conv_out[:, 2 * QK:], projected[4], projected[5], decay_log, dt_bias, DH)
        local_out, query_eff, transfer, offset_map = span_terms(queries.transpose(1, 0, 2), key_rows.transpose(1, 0, 2), values.transpose(1, 0, 2), beta_gate.T, log_decay.T)
        core = local_out + jnp.einsum('htk,hvk->htv', query_eff, state, precision=highest)
        new_state = jnp.einsum('hvk,hkj->hvj', state, transfer, precision=highest) + offset_map
        gated = gate_norm(core.transpose(1, 0, 2), projected[3], norm_gain)
        grouped = gated.astype(jnp.float32).reshape(SPAN, N_FSDP, VW // N_FSDP)
        partial_terms = jnp.einsum('cgu,gud->gcd', grouped, out_groups, precision=highest).astype(jnp.bfloat16)
        block_out = lax.optimization_barrier(jnp.sum(partial_terms.astype(jnp.float32), axis=0)).astype(jnp.bfloat16)
        return ((new_state, mixed_rows[mixed_rows.shape[0] - (KCONV - 1):]), block_out)
    start_state = (jnp.zeros((HV, DH, DH), jnp.float32), jnp.zeros((KCONV - 1, 2 * QK + VW), jnp.bfloat16))
    final_state, outputs = lax.scan(advance, start_state, tok_blocks)
    return outputs.reshape(TOKENS, D)
```

```python
import functools

import jax
import jax.numpy as jnp
from jax import lax
from jax.experimental import pallas as pl
from jax.experimental.pallas import tpu as pltpu
from jax.sharding import PartitionSpec as P

MESH = pl.DeviceIdType.MESH
F32 = jnp.float32
BF16 = jnp.bfloat16
ANY = pl.BlockSpec(memory_space=pl.ANY)
VMEM = pl.BlockSpec(memory_space=pltpu.VMEM)
SMEM = pl.BlockSpec(memory_space=pltpu.SMEM)
DMA = pltpu.SemaphoreType.DMA

D = 2048
DSH = 512
TOK = 128
BLK = 512
HALO = 16
ROWS = HALO + BLK
GQ, GV = 256, 512
GC = 2 * GQ + 2 * GV
DH = 128
NH = 4
NCH = BLK // DH
NSEQ = 32


def coords():
    seq, fsdp = lax.axis_index("seq"), lax.axis_index("fsdp")
    return seq, fsdp, seq % 2, fsdp // 2, fsdp % 2


def gather_kernel(
    tok_ref, wq_ref, wk_ref, wv_ref, wz_ref, wba_ref, tok_out, w_out, wba_out, send, recv, loc
):
    seq, fsdp, zlo, zhi, core = coords()
    base = seq - zlo
    sibling = zhi * 2 + 1 - core
    far = (1 - zhi) * 2
    last = fsdp == 3

    near, cross = far + core, far + 1 - core
    weight_peers = [(seq, sibling), (base + 1 - zlo, near), (base + 1 - zlo, cross)]
    token_peers = [(seq, sibling), (seq, near), (seq, cross)]
    signalled = [weight_peers[0]] + weight_peers[1:] + token_peers[1:]

    barrier = pltpu.get_barrier_semaphore()
    for peer in signalled:
        pl.semaphore_signal(barrier, inc=1, device_id=peer, device_id_type=MESH)

    @pl.when(seq > 0)
    def _():
        pl.semaphore_signal(barrier, inc=1, device_id=(seq - 1, 3), device_id_type=MESH)

    sends_halo = jnp.logical_and(last, seq < NSEQ - 1)
    pl.semaphore_wait(barrier, 5 + 4 * sends_halo.astype(jnp.int32))

    def weight_pieces(group):
        q_at = pl.multiple_of(group * GQ, GQ)
        v_at = pl.multiple_of(group * GV, GV)
        return [
            (wq_ref.at[:, pl.ds(q_at, GQ)], w_out.at[fsdp, :, pl.ds(0, GQ)]),
            (wk_ref.at[:, pl.ds(q_at, GQ)], w_out.at[fsdp, :, pl.ds(GQ, GQ)]),
            (wv_ref.at[:, pl.ds(v_at, GV)], w_out.at[fsdp, :, pl.ds(2 * GQ, GV)]),
            (wz_ref.at[:, pl.ds(v_at, GV)], w_out.at[fsdp, :, pl.ds(2 * GQ + GV, GV)]),
            (wba_ref, wba_out.at[fsdp]),
        ]

    started = []
    index = 0
    for peer in token_peers:
        copy = pltpu.make_async_remote_copy(
            tok_ref,
            tok_out.at[pl.ds(pl.multiple_of(HALO + fsdp * TOK, 16), TOK)],
            send.at[index],
            recv.at[index],
            device_id=peer,
            device_id_type=MESH,
        )
        copy.start()
        started.append(copy)
        index += 1
    for peer in weight_peers:
        for source, target in weight_pieces(peer[1]):
            copy = pltpu.make_async_remote_copy(
                source, target, send.at[index], recv.at[index], device_id=peer, device_id_type=MESH
            )
            copy.start()
            started.append(copy)
            index += 1

    def halo_copy(k):
        return pltpu.make_async_remote_copy(
            tok_ref.at[pl.ds(TOK - HALO, HALO)],
            tok_out.at[pl.ds(0, HALO)],
            send.at[index + k],
            recv.at[index],
            device_id=(lax.rem(seq + 1, NSEQ), k),
            device_id_type=MESH,
        )

    @pl.when(sends_halo)
    def _():
        for k in range(4):
            halo_copy(k).start()

    local = [
        (tok_ref, tok_out.at[pl.ds(pl.multiple_of(HALO + fsdp * TOK, 16), TOK)])
    ] + weight_pieces(fsdp)
    copies = []
    for i, (source, target) in enumerate(local):
        copy = pltpu.make_async_copy(source, target, loc.at[i])
        copy.start()
        copies.append(copy)
    for copy in copies:
        copy.wait()
    for copy in started:
        copy.wait()

    @pl.when(sends_halo)
    def _():
        for k in range(4):
            halo_copy(k).wait_send()

    @pl.when(seq > 0)
    def _():
        halo_copy(0).wait_recv()


def gather(tokens, w_query, w_key, w_value, w_gate, wba):
    count = 3 + 15 + 4
    return pl.pallas_call(
        gather_kernel,
        out_shape=(
            jax.ShapeDtypeStruct((ROWS, D), BF16),
            jax.ShapeDtypeStruct((4, DSH, GC), BF16),
            jax.ShapeDtypeStruct((4, 32, DSH), BF16),
        ),
        in_specs=[ANY] * 6,
        out_specs=(ANY, ANY, ANY),
        scratch_shapes=[DMA((count,)), DMA((count,)), DMA((6,))],
        compiler_params=pltpu.CompilerParams(collective_id=0, has_side_effects=True),
        name="gather",
    )(tokens, w_query, w_key, w_value, w_gate, wba)


def nn(a, b):
    return jnp.dot(a.astype(BF16), b.astype(BF16), preferred_element_type=F32)


def nt(a, b):
    return lax.dot_general(
        a.astype(BF16), b.astype(BF16), (((1,), (1,)), ((), ())), preferred_element_type=F32
    )


def tn(a, b):
    return lax.dot_general(
        a.astype(BF16), b.astype(BF16), (((0,), (0,)), ((), ())), preferred_element_type=F32
    )


def full(a, b):
    return jnp.dot(a, b, preferred_element_type=F32, precision=lax.Precision.HIGHEST)


def split(a):
    high = a.astype(BF16)
    return high, (a - high.astype(F32)).astype(BF16)


def fine(a, b):
    ah, al = split(a)
    bh, bl = split(b)
    dot = functools.partial(jnp.dot, preferred_element_type=F32)
    return dot(ah, bh) + dot(al, bh) + dot(ah, bl)


INV = nn


def silu(v):
    return v / (1.0 + jnp.exp(-v))


def local_kernel(
    tok_ref, w_ref, wba_ref, conv_ref, rate_ref, bias_ref,
    core_ref, qt_ref, gate_ref, map_ref,
    mixed, act, small, chain,
):
    seq, fsdp, _, _, _ = coords()

    def project(j):
        total = None
        for part in range(4):
            term = jnp.dot(
                tok_ref[:, pl.ds(part * DSH, DSH)],
                w_ref[part, :, pl.ds(j * 256, 256)],
                preferred_element_type=F32,
            )
            total = term if total is None else total + term
        return total

    for j in range(4):
        mixed[...] = project(j).astype(BF16).astype(F32)

        @pl.when(seq == 0)
        def _():
            mixed[pl.ds(0, HALO), :] = jnp.zeros((HALO, 256), F32)

        if j < 2:
            at = j * 1024 + fsdp * GQ
        else:
            at = 2048 + fsdp * GV + (j - 2) * 256
        taps = conv_ref[:, pl.ds(pl.multiple_of(at, 256), 256)].astype(F32)
        total = taps[0:1, :] * mixed[pl.ds(HALO - 3, BLK), :]
        for i in range(1, 4):
            total = total + taps[i : i + 1, :] * mixed[pl.ds(HALO - 3 + i, BLK), :]
        out = silu(total).astype(BF16).astype(F32)
        for part in range(2):
            head = out[:, part * DH : (part + 1) * DH]
            if j < 2:
                head = head * lax.rsqrt(jnp.sum(head * head, axis=-1, keepdims=True) + 1e-6)
                if j == 0:
                    head = head * DH**-0.5
            act[2 * j + part] = head
    for j in range(2):
        gate_ref[:, pl.ds(j * 256, 256)] = project(4 + j)[HALO:].astype(BF16)

    row = lax.broadcasted_iota(jnp.int32, (8, 32), 0)
    col = lax.broadcasted_iota(jnp.int32, (8, 32), 1)
    pick = (col == jnp.where(row < 4, 0, 12) + fsdp * 4 + row).astype(BF16)
    rows = None
    for part in range(4):
        own = jnp.dot(pick, wba_ref[part], preferred_element_type=F32).astype(BF16)
        term = lax.dot_general(
            own, tok_ref[pl.ds(HALO, BLK), pl.ds(part * DSH, DSH)],
            (((1,), (1,)), ((), ())), preferred_element_type=F32,
        )
        rows = term if rows is None else rows + term
    rows = rows.astype(BF16).astype(F32)
    beta_rows = jax.nn.sigmoid(rows[0:4])
    which = lax.broadcasted_iota(jnp.int32, (4, 1), 0)
    rate = jnp.zeros((4, 1), F32)
    bias = jnp.zeros((4, 1), F32)
    for h in range(4):
        rate = jnp.where(which == h, rate_ref[fsdp * 4 + h], rate)
        bias = jnp.where(which == h, bias_ref[fsdp * 4 + h], bias)
    decay_rows = -jnp.exp(rate) * jax.nn.softplus(rows[4:8] + bias)
    small[...] = jnp.concatenate([decay_rows, beta_rows], axis=0)

    at_row = lax.broadcasted_iota(jnp.int32, (DH, DH), 0)
    at_col = lax.broadcasted_iota(jnp.int32, (DH, DH), 1)
    strict = at_row > at_col
    within = at_row >= at_col
    eye = (at_row == at_col).astype(F32)
    upper = (at_row <= at_col).astype(F32)

    def level(size):
        return jnp.logical_and(
            at_row // (2 * size) == at_col // (2 * size),
            jnp.logical_and(at_row % (2 * size) >= size, at_col % (2 * size) < size),
        )

    base = jnp.logical_and(strict, at_row // 8 == at_col // 8)

    for h in range(NH):
        chain[h, 0:DH] = eye
        chain[h, DH:] = jnp.zeros((DH, DH), F32)

    def chunk(n, carry):
        tokens = pl.ds(pl.multiple_of(n * DH, DH), DH)
        pair = small[:, tokens]
        cumul_rows = full(pair, upper)
        columns = jnp.concatenate([cumul_rows[0:4], pair[4:8]], axis=0).T
        for kh in range(2):
            q = act[kh, tokens, :]
            k = act[2 + kh, tokens, :]
            kk = nt(k, k)
            qk = nt(q, k)
            for h in (2 * kh, 2 * kh + 1):
                v = act[4 + h, tokens, :]
                c = columns[:, h : h + 1]
                b = columns[:, 4 + h : 5 + h]
                last = cumul_rows[h : h + 1, DH - 1 : DH]
                fall = jnp.where(within, jnp.exp(jnp.where(within, c - cumul_rows[h : h + 1, :], 0.0)), 0.0)
                a = jnp.where(strict, b * kk * fall, 0.0)
                scores = qk * fall
                a1 = jnp.where(base, a, 0.0)
                a2 = INV(a1, a1)
                a34 = INV(jnp.concatenate([a1, a2], axis=0), a2)
                x = eye - a1 + a2 - a34[:DH]
                x = x + INV(x, a34[DH:])
                for size in (8, 16, 32, 64):
                    x = x - INV(INV(x, jnp.where(level(size), a, 0.0)), x)
                grow = jnp.exp(c)
                right = jnp.concatenate([b * v, (b * grow) * k], axis=1)
                solved = nn(x, right)
                seen = nn(scores, solved)
                query_eff = grow * q - seen[:, DH:]
                tail = jnp.exp(last - c)
                maps = tn(solved * tail, k)
                transfer = jnp.exp(last) * eye - maps[DH:]
                offset = maps[:DH]
                before = chain[h]
                both = nt(query_eff, before)
                qt_ref[h, tokens, :] = both[:, :DH].astype(BF16)
                core_ref[h, tokens, :] = seen[:, :DH] + both[:, DH:]
                after = nn(before, transfer)
                chain[h, 0:DH] = after[0:DH]
                chain[h, DH:] = after[DH:] + offset
        return carry

    lax.fori_loop(0, NCH, chunk, 0)
    map_ref[...] = chain[...]


def local_terms(tok_all, w_all, wba_all, conv_weight, decay_log, dt_bias):
    return pl.pallas_call(
        local_kernel,
        out_shape=(
            jax.ShapeDtypeStruct((NH, BLK, DH), F32),
            jax.ShapeDtypeStruct((NH, BLK, DH), BF16),
            jax.ShapeDtypeStruct((BLK, GV), BF16),
            jax.ShapeDtypeStruct((NH, 2 * DH, DH), F32),
        ),
        in_specs=[VMEM, VMEM, VMEM, VMEM, SMEM, SMEM],
        out_specs=(VMEM, VMEM, VMEM, VMEM),
        scratch_shapes=[
            pltpu.VMEM((ROWS, 256), F32),
            pltpu.VMEM((8, BLK, DH), F32),
            pltpu.VMEM((8, BLK), F32),
            pltpu.VMEM((NH, 2 * DH, DH), F32),
        ],
        compiler_params=pltpu.CompilerParams(vmem_limit_bytes=48 << 20),
        name="local_terms",
    )(tok_all, w_all, wba_all, conv_weight, decay_log, dt_bias)


ROUNDS = 5


def scan_kernel(map_ref, state_ref, outgoing, arrived, window, before, send, recv):
    seq, fsdp = lax.axis_index("seq"), lax.axis_index("fsdp")
    barrier = pltpu.get_barrier_semaphore()
    for r in range(ROUNDS):
        @pl.when(seq >= 2**r)
        def _():
            pl.semaphore_signal(
                barrier, inc=1, device_id=(seq - 2**r, fsdp), device_id_type=MESH
            )
    targets = sum((seq + 2**r < NSEQ).astype(jnp.int32) for r in range(ROUNDS))

    @pl.when(targets > 0)
    def _():
        pl.semaphore_wait(barrier, targets)

    def copy(r, h):
        return pltpu.make_async_remote_copy(
            outgoing.at[r, h], arrived.at[r, h], send.at[r, h], recv.at[r, h],
            device_id=(lax.rem(seq + 2**r, NSEQ), fsdp), device_id_type=MESH,
        )

    def compose(earlier, later):
        high, low = split(later[0:DH])
        dot = functools.partial(jnp.dot, preferred_element_type=F32)
        out = dot(earlier, high) + dot(earlier, low)
        return out[0:DH], out[DH:] + later[DH:]

    for h in range(NH):
        outgoing[0, h] = map_ref[h].astype(BF16)

        @pl.when(seq + 1 < NSEQ)
        def _():
            copy(0, h).start()

        window[h] = map_ref[h]
        before[h, 0:DH] = jnp.zeros((DH, DH), F32)
        before[h, DH:] = jnp.zeros((DH, DH), F32)

    for r in range(ROUNDS):
        step = 2**r
        for h in range(NH):
            @pl.when(seq >= step)
            def _():
                copy(r, h).wait_recv()
                if r < ROUNDS - 1:
                    top, low = compose(arrived[r, h], window[h])
                    window[h, 0:DH] = top
                    window[h, DH:] = low

            if r < ROUNDS - 1:
                outgoing[r + 1, h] = window[h].astype(BF16)

                @pl.when(seq + 2 * step < NSEQ)
                def _():
                    copy(r + 1, h).start()

            @pl.when(seq >= step)
            def _():
                if r == 0:
                    before[h] = arrived[r, h].astype(F32)
                else:
                    top, low = compose(arrived[r, h], before[h])
                    before[h, 0:DH] = top
                    before[h, DH:] = low

    for h in range(NH):
        state_ref[h] = before[h, DH:]
    for r in range(ROUNDS):
        @pl.when(seq + 2**r < NSEQ)
        def _():
            for h in range(NH):
                copy(r, h).wait_send()


def scan_states(maps):
    return pl.pallas_call(
        scan_kernel,
        out_shape=jax.ShapeDtypeStruct((NH, DH, DH), F32),
        in_specs=[VMEM],
        out_specs=VMEM,
        scratch_shapes=[
            pltpu.VMEM((ROUNDS, NH, 2 * DH, DH), BF16),
            pltpu.VMEM((ROUNDS, NH, 2 * DH, DH), BF16),
            pltpu.VMEM((NH, 2 * DH, DH), F32),
            pltpu.VMEM((NH, 2 * DH, DH), F32),
            DMA((ROUNDS, NH)),
            DMA((ROUNDS, NH)),
        ],
        compiler_params=pltpu.CompilerParams(
            collective_id=1, has_side_effects=True, vmem_limit_bytes=24 << 20
        ),
        name="scan_states",
    )(maps)


def output_kernel(core_ref, qt_ref, gate_ref, state_ref, gain_ref, wout_ref, out_ref, gated):
    gain = gain_ref[...].reshape(1, DH)
    for h in range(NH):
        core = core_ref[h] + nt(qt_ref[h], state_ref[h])
        scale = lax.rsqrt(jnp.mean(core * core, axis=-1, keepdims=True) + 1e-6)
        z = gate_ref[:, pl.ds(h * DH, DH)].astype(F32)
        gated[:, pl.ds(h * DH, DH)] = (core * scale * gain * silu(z)).astype(BF16)
    for j in range(D // 256):
        out_ref[:, pl.ds(j * 256, 256)] = jnp.dot(
            gated[...], wout_ref[:, pl.ds(j * 256, 256)], preferred_element_type=F32
        ).astype(BF16)


def output_terms(core, qt, gate, states, norm_gain, w_out):
    return pl.pallas_call(
        output_kernel,
        out_shape=jax.ShapeDtypeStruct((BLK, D), BF16),
        in_specs=[VMEM] * 6,
        out_specs=VMEM,
        scratch_shapes=[pltpu.VMEM((BLK, GV), BF16)],
        compiler_params=pltpu.CompilerParams(vmem_limit_bytes=40 << 20),
        name="output_terms",
    )(core, qt, gate, states, norm_gain, w_out)


def scatter_kernel(term_ref, out_ref, arrived, send, recv):
    seq, fsdp, _, zhi, core = coords()
    peers = [zhi * 2 + 1 - core, (1 - zhi) * 2 + core, (1 - zhi) * 2 + 1 - core]
    barrier = pltpu.get_barrier_semaphore()
    for peer in peers:
        pl.semaphore_signal(barrier, inc=1, device_id=(seq, peer), device_id_type=MESH)
    pl.semaphore_wait(barrier, 3)
    copies = []
    for i, peer in enumerate(peers):
        copy = pltpu.make_async_remote_copy(
            term_ref.at[pl.ds(pl.multiple_of(peer * TOK, TOK), TOK)],
            arrived.at[i], send.at[i], recv.at[i],
            device_id=(seq, peer), device_id_type=MESH,
        )
        copy.start()
        copies.append(copy)
    for copy in copies:
        copy.wait()
    total = term_ref[pl.ds(pl.multiple_of(fsdp * TOK, TOK), TOK), :].astype(F32)
    for i in range(3):
        total = total + arrived[i].astype(F32)
    out_ref[...] = total.astype(BF16)


def scatter(terms):
    return pl.pallas_call(
        scatter_kernel,
        out_shape=jax.ShapeDtypeStruct((TOK, D), BF16),
        in_specs=[VMEM],
        out_specs=VMEM,
        scratch_shapes=[pltpu.VMEM((3, TOK, D), BF16), DMA((3,)), DMA((3,))],
        compiler_params=pltpu.CompilerParams(
            collective_id=2, has_side_effects=True, vmem_limit_bytes=24 << 20
        ),
        name="scatter",
    )(terms)


def shards(
    tokens, w_query, w_key, w_value, w_gate_out, w_beta, w_decay,
    conv_weight, decay_log, dt_bias, norm_gain, w_out,
):
    wba = jnp.concatenate([w_beta, w_decay], axis=1).T
    tok_all, w_all, wba_all = gather(tokens, w_query, w_key, w_value, w_gate_out, wba)
    core, qt, gate, maps = local_terms(tok_all, w_all, wba_all, conv_weight, decay_log, dt_bias)
    states = scan_states(maps)
    terms = output_terms(core, qt, gate, states, norm_gain, w_out)
    return scatter(terms)


def solution(mesh):
    return jax.shard_map(
        shards,
        mesh=mesh,
        in_specs=(
            P(("seq", "fsdp"), None),
            P("fsdp", None), P("fsdp", None), P("fsdp", None), P("fsdp", None),
            P("fsdp", None), P("fsdp", None),
            P(), P(), P(), P(),
            P("fsdp", None),
        ),
        out_specs=P(("seq", "fsdp"), None),
        check_vma=False,
    )
```

```python
import functools

import jax
import jax.numpy as jnp
from jax import lax
from jax.experimental import pallas as pl
from jax.experimental.pallas import tpu as pltpu
from jax.sharding import PartitionSpec as P

MESH = pl.DeviceIdType.MESH
F32 = jnp.float32
BF16 = jnp.bfloat16
ANY = pl.BlockSpec(memory_space=pl.ANY)
VMEM = pl.BlockSpec(memory_space=pltpu.VMEM)
SMEM = pl.BlockSpec(memory_space=pltpu.SMEM)
DMA = pltpu.SemaphoreType.DMA

D = 2048
DSH = 512
TOK = 128
BLK = 512
HALO = 16
ROWS = HALO + BLK
GQ, GV = 256, 512
GC = 2 * GQ + 2 * GV
DH = 128
NH = 4
NCH = BLK // DH
NSEQ = 32


def coords():
    seq, fsdp = lax.axis_index("seq"), lax.axis_index("fsdp")
    return seq, fsdp, seq % 2, fsdp // 2, fsdp % 2


SECTIONS = ((0, GQ), (GQ, GQ), (2 * GQ, GV), (2 * GQ + GV, GV))
PIECE = DSH // 4


def gather_kernel(
    tok_ref, wq_ref, wk_ref, wv_ref, wz_ref, wba_ref, tok_out, w_out, wba_out,
    tok_send, tok_recv, ba_send, ba_recv, near_send, near_recv, cut_send, cut_recv,
    ring_send, ring_recv, loc,
):
    seq, fsdp, zlo, zhi, core = coords()
    x, y = seq // 8, (seq // 2) % 4
    sibling = (seq, zhi * 2 + 1 - core)
    far = (1 - zhi) * 2
    across = (seq, far + core)
    partner = seq - zlo + 1 - zlo
    partners = [(partner, far + core), (partner, far + 1 - core)]
    rings = [
        [(lax.rem(x + d, 4) * 8 + y * 2 + zlo, fsdp) for d in (1, 3, 2)],
        [(x * 8 + lax.rem(y + d, 4) * 2 + zlo, fsdp) for d in (1, 3, 2)],
    ]
    sends_halo = jnp.logical_and(fsdp == 3, seq < NSEQ - 1)

    barrier = pltpu.get_barrier_semaphore()
    for peer in [sibling, across] + partners + rings[0] + rings[1]:
        pl.semaphore_signal(barrier, inc=1, device_id=peer, device_id_type=MESH)

    @pl.when(seq > 0)
    def _():
        pl.semaphore_signal(barrier, inc=1, device_id=(seq - 1, 3), device_id_type=MESH)

    pl.semaphore_wait(barrier, 10 + 4 * sends_halo.astype(jnp.int32))

    def remote(source, target, send, recv, peer):
        return pltpu.make_async_remote_copy(
            source, target, send, recv, device_id=peer, device_id_type=MESH
        )

    def token_rows(group):
        return tok_out.at[pl.ds(pl.multiple_of(HALO + group * TOK, 16), TOK)]

    weights = (wq_ref, wk_ref, wv_ref, wz_ref)

    def columns(section, group):
        width = SECTIONS[section][1]
        return pl.ds(pl.multiple_of(group * width, width), width)

    def held(shard, rows, section):
        start, width = SECTIONS[section]
        return w_out.at[shard, rows, pl.ds(start, width)]

    all_rows = pl.ds(0, DSH)

    tok_copies = [
        remote(tok_ref, token_rows(fsdp), tok_send.at[i], tok_recv.at[i], peer)
        for i, peer in enumerate((across, sibling))
    ]
    for copy in tok_copies:
        copy.start()

    def halo_copy(k):
        return remote(
            tok_ref.at[pl.ds(TOK - HALO, HALO)], tok_out.at[pl.ds(0, HALO)],
            tok_send.at[3 + k], tok_recv.at[3], (lax.rem(seq + 1, NSEQ), k),
        )

    @pl.when(sends_halo)
    def _():
        for k in range(4):
            halo_copy(k).start()

    piece_at = jnp.where(core == 0, x, y)
    own_piece = pl.ds(pl.multiple_of(piece_at * PIECE, PIECE), PIECE)

    def cut_copy(section, i):
        peer = partners[i]
        return remote(
            weights[section].at[own_piece, columns(section, peer[1])],
            held(fsdp, own_piece, section),
            cut_send.at[i, section], cut_recv.at[core, section], peer,
        )

    for section in range(4):
        for i in range(2):
            cut_copy(section, i).start()

    ba_copies = [
        remote(wba_ref, wba_out.at[fsdp], ba_send.at[i], ba_recv.at[i], peer)
        for i, peer in enumerate([sibling] + partners)
    ]
    for copy in ba_copies:
        copy.start()

    near_copies = [
        remote(
            weights[section].at[:, columns(section, sibling[1])],
            held(fsdp, all_rows, section),
            near_send.at[section], near_recv.at[section], sibling,
        )
        for section in range(4)
    ]
    for copy in near_copies:
        copy.start()

    local = [(tok_ref, token_rows(fsdp)), (wba_ref, wba_out.at[fsdp])] + [
        (weights[section].at[:, columns(section, fsdp)], held(fsdp, all_rows, section))
        for section in range(4)
    ]
    local_copies = [
        pltpu.make_async_copy(source, target, loc.at[i])
        for i, (source, target) in enumerate(local)
    ]
    for copy in local_copies:
        copy.start()

    tok_copies[0].wait_recv()
    pass_on = remote(
        token_rows(across[1]), token_rows(across[1]), tok_send.at[2], tok_recv.at[2], sibling
    )
    pass_on.start()

    places = [x, y]

    def ring_copy(section, shard, i):
        rows = pl.ds(pl.multiple_of(places[shard] * PIECE, PIECE), PIECE)
        block = held(far + shard, rows, section)
        return remote(
            block, block, ring_send.at[shard, i, section], ring_recv.at[shard, i, section],
            rings[shard][i],
        )

    for section in range(4):
        for shard in range(2):
            rows = pl.ds(pl.multiple_of(places[shard] * PIECE, PIECE), PIECE)
            block = held(far + shard, rows, section)
            remote(
                block, block, cut_send.at[0, section], cut_recv.at[shard, section], partners[0]
            ).wait_recv()
            for i in range(3):
                ring_copy(section, shard, i).start()

    for copy in local_copies:
        copy.wait()
    tok_copies[0].wait_send()
    tok_copies[1].wait()
    pass_on.wait()
    for copy in ba_copies + near_copies:
        copy.wait()
    for section in range(4):
        for i in range(2):
            cut_copy(section, i).wait_send()
        for shard in range(2):
            for i in range(3):
                ring_copy(section, shard, i).wait()

    @pl.when(sends_halo)
    def _():
        for k in range(4):
            halo_copy(k).wait_send()

    @pl.when(seq > 0)
    def _():
        halo_copy(0).wait_recv()


def gather(tokens, w_query, w_key, w_value, w_gate, wba):
    return pl.pallas_call(
        gather_kernel,
        out_shape=(
            jax.ShapeDtypeStruct((ROWS, D), BF16),
            jax.ShapeDtypeStruct((4, DSH, GC), BF16),
            jax.ShapeDtypeStruct((4, 32, DSH), BF16),
        ),
        in_specs=[ANY] * 6,
        out_specs=(ANY, ANY, ANY),
        scratch_shapes=[
            DMA((7,)), DMA((4,)), DMA((3,)), DMA((3,)), DMA((4,)), DMA((4,)),
            DMA((2, 4)), DMA((2, 4)), DMA((2, 3, 4)), DMA((2, 3, 4)), DMA((6,)),
        ],
        compiler_params=pltpu.CompilerParams(collective_id=0, has_side_effects=True),
        name="gather",
    )(tokens, w_query, w_key, w_value, w_gate, wba)


def nn(a, b):
    return jnp.dot(a.astype(BF16), b.astype(BF16), preferred_element_type=F32)


def nt(a, b):
    return lax.dot_general(
        a.astype(BF16), b.astype(BF16), (((1,), (1,)), ((), ())), preferred_element_type=F32
    )


def tn(a, b):
    return lax.dot_general(
        a.astype(BF16), b.astype(BF16), (((0,), (0,)), ((), ())), preferred_element_type=F32
    )


def full(a, b):
    return jnp.dot(a, b, preferred_element_type=F32, precision=lax.Precision.HIGHEST)


def split(a):
    high = a.astype(BF16)
    return high, (a - high.astype(F32)).astype(BF16)


def fine(a, b):
    ah, al = split(a)
    bh, bl = split(b)
    dot = functools.partial(jnp.dot, preferred_element_type=F32)
    return dot(ah, bh) + dot(al, bh) + dot(ah, bl)


INV = nn


def silu(v):
    return v / (1.0 + jnp.exp(-v))


def local_kernel(
    tok_ref, w_ref, wba_ref, conv_ref, rate_ref, bias_ref,
    core_ref, qt_ref, gate_ref, map_ref,
    mixed, act, small, chain,
):
    seq, fsdp, _, _, _ = coords()

    def project(j):
        total = None
        for part in range(4):
            term = jnp.dot(
                tok_ref[:, pl.ds(part * DSH, DSH)],
                w_ref[part, :, pl.ds(j * 256, 256)],
                preferred_element_type=F32,
            )
            total = term if total is None else total + term
        return total

    for j in range(4):
        mixed[...] = project(j).astype(BF16).astype(F32)

        @pl.when(seq == 0)
        def _():
            mixed[pl.ds(0, HALO), :] = jnp.zeros((HALO, 256), F32)

        if j < 2:
            at = j * 1024 + fsdp * GQ
        else:
            at = 2048 + fsdp * GV + (j - 2) * 256
        taps = conv_ref[:, pl.ds(pl.multiple_of(at, 256), 256)].astype(F32)
        total = taps[0:1, :] * mixed[pl.ds(HALO - 3, BLK), :]
        for i in range(1, 4):
            total = total + taps[i : i + 1, :] * mixed[pl.ds(HALO - 3 + i, BLK), :]
        out = silu(total).astype(BF16).astype(F32)
        for part in range(2):
            head = out[:, part * DH : (part + 1) * DH]
            if j < 2:
                head = head * lax.rsqrt(jnp.sum(head * head, axis=-1, keepdims=True) + 1e-6)
                if j == 0:
                    head = head * DH**-0.5
            act[2 * j + part] = head
    for j in range(2):
        gate_ref[:, pl.ds(j * 256, 256)] = project(4 + j)[HALO:].astype(BF16)

    row = lax.broadcasted_iota(jnp.int32, (8, 32), 0)
    col = lax.broadcasted_iota(jnp.int32, (8, 32), 1)
    pick = (col == jnp.where(row < 4, 0, 12) + fsdp * 4 + row).astype(BF16)
    rows = None
    for part in range(4):
        own = jnp.dot(pick, wba_ref[part], preferred_element_type=F32).astype(BF16)
        term = lax.dot_general(
            own, tok_ref[pl.ds(HALO, BLK), pl.ds(part * DSH, DSH)],
            (((1,), (1,)), ((), ())), preferred_element_type=F32,
        )
        rows = term if rows is None else rows + term
    rows = rows.astype(BF16).astype(F32)
    beta_rows = jax.nn.sigmoid(rows[0:4])
    which = lax.broadcasted_iota(jnp.int32, (4, 1), 0)
    rate = jnp.zeros((4, 1), F32)
    bias = jnp.zeros((4, 1), F32)
    for h in range(4):
        rate = jnp.where(which == h, rate_ref[fsdp * 4 + h], rate)
        bias = jnp.where(which == h, bias_ref[fsdp * 4 + h], bias)
    decay_rows = -jnp.exp(rate) * jax.nn.softplus(rows[4:8] + bias)
    small[...] = jnp.concatenate([decay_rows, beta_rows], axis=0)

    at_row = lax.broadcasted_iota(jnp.int32, (DH, DH), 0)
    at_col = lax.broadcasted_iota(jnp.int32, (DH, DH), 1)
    strict = at_row > at_col
    within = at_row >= at_col
    eye = (at_row == at_col).astype(F32)
    upper = (at_row <= at_col).astype(F32)

    def level(size):
        return jnp.logical_and(
            at_row // (2 * size) == at_col // (2 * size),
            jnp.logical_and(at_row % (2 * size) >= size, at_col % (2 * size) < size),
        )

    base = jnp.logical_and(strict, at_row // 8 == at_col // 8)

    for h in range(NH):
        chain[h, 0:DH] = eye
        chain[h, DH:] = jnp.zeros((DH, DH), F32)

    def chunk(n, carry):
        tokens = pl.ds(pl.multiple_of(n * DH, DH), DH)
        pair = small[:, tokens]
        cumul_rows = full(pair, upper)
        columns = jnp.concatenate([cumul_rows[0:4], pair[4:8]], axis=0).T
        for kh in range(2):
            q = act[kh, tokens, :]
            k = act[2 + kh, tokens, :]
            kk = nt(k, k)
            qk = nt(q, k)
            for h in (2 * kh, 2 * kh + 1):
                v = act[4 + h, tokens, :]
                c = columns[:, h : h + 1]
                b = columns[:, 4 + h : 5 + h]
                last = cumul_rows[h : h + 1, DH - 1 : DH]
                fall = jnp.where(within, jnp.exp(jnp.where(within, c - cumul_rows[h : h + 1, :], 0.0)), 0.0)
                a = jnp.where(strict, b * kk * fall, 0.0)
                scores = qk * fall
                a1 = jnp.where(base, a, 0.0)
                a2 = INV(a1, a1)
                a34 = INV(jnp.concatenate([a1, a2], axis=0), a2)
                x = eye - a1 + a2 - a34[:DH]
                x = x + INV(x, a34[DH:])
                for size in (8, 16, 32, 64):
                    x = x - INV(INV(x, jnp.where(level(size), a, 0.0)), x)
                grow = jnp.exp(c)
                right = jnp.concatenate([b * v, (b * grow) * k], axis=1)
                solved = nn(x, right)
                seen = nn(scores, solved)
                query_eff = grow * q - seen[:, DH:]
                tail = jnp.exp(last - c)
                maps = tn(solved * tail, k)
                transfer = jnp.exp(last) * eye - maps[DH:]
                offset = maps[:DH]
                before = chain[h]
                both = nt(query_eff, before)
                qt_ref[h, tokens, :] = both[:, :DH].astype(BF16)
                core_ref[h, tokens, :] = seen[:, :DH] + both[:, DH:]
                after = nn(before, transfer)
                chain[h, 0:DH] = after[0:DH]
                chain[h, DH:] = after[DH:] + offset
        return carry

    lax.fori_loop(0, NCH, chunk, 0)
    map_ref[...] = chain[...]


def local_terms(tok_all, w_all, wba_all, conv_weight, decay_log, dt_bias):
    return pl.pallas_call(
        local_kernel,
        out_shape=(
            jax.ShapeDtypeStruct((NH, BLK, DH), F32),
            jax.ShapeDtypeStruct((NH, BLK, DH), BF16),
            jax.ShapeDtypeStruct((BLK, GV), BF16),
            jax.ShapeDtypeStruct((NH, 2 * DH, DH), F32),
        ),
        in_specs=[VMEM, VMEM, VMEM, VMEM, SMEM, SMEM],
        out_specs=(VMEM, VMEM, VMEM, VMEM),
        scratch_shapes=[
            pltpu.VMEM((ROWS, 256), F32),
            pltpu.VMEM((8, BLK, DH), F32),
            pltpu.VMEM((8, BLK), F32),
            pltpu.VMEM((NH, 2 * DH, DH), F32),
        ],
        compiler_params=pltpu.CompilerParams(vmem_limit_bytes=48 << 20),
        name="local_terms",
    )(tok_all, w_all, wba_all, conv_weight, decay_log, dt_bias)


ROUNDS = 5


def scan_kernel(map_ref, state_ref, outgoing, arrived, window, before, send, recv):
    seq, fsdp = lax.axis_index("seq"), lax.axis_index("fsdp")
    barrier = pltpu.get_barrier_semaphore()
    for r in range(ROUNDS):
        @pl.when(seq >= 2**r)
        def _():
            pl.semaphore_signal(
                barrier, inc=1, device_id=(seq - 2**r, fsdp), device_id_type=MESH
            )
    targets = sum((seq + 2**r < NSEQ).astype(jnp.int32) for r in range(ROUNDS))

    @pl.when(targets > 0)
    def _():
        pl.semaphore_wait(barrier, targets)

    def copy(r, h):
        return pltpu.make_async_remote_copy(
            outgoing.at[r, h], arrived.at[r, h], send.at[r, h], recv.at[r, h],
            device_id=(lax.rem(seq + 2**r, NSEQ), fsdp), device_id_type=MESH,
        )

    def compose(earlier, later):
        high, low = split(later[0:DH])
        dot = functools.partial(jnp.dot, preferred_element_type=F32)
        out = dot(earlier, high) + dot(earlier, low)
        return out[0:DH], out[DH:] + later[DH:]

    for h in range(NH):
        outgoing[0, h] = map_ref[h].astype(BF16)

        @pl.when(seq + 1 < NSEQ)
        def _():
            copy(0, h).start()

        window[h] = map_ref[h]
        before[h, 0:DH] = jnp.zeros((DH, DH), F32)
        before[h, DH:] = jnp.zeros((DH, DH), F32)

    for r in range(ROUNDS):
        step = 2**r
        for h in range(NH):
            @pl.when(seq >= step)
            def _():
                copy(r, h).wait_recv()
                if r < ROUNDS - 1:
                    top, low = compose(arrived[r, h], window[h])
                    window[h, 0:DH] = top
                    window[h, DH:] = low

            if r < ROUNDS - 1:
                outgoing[r + 1, h] = window[h].astype(BF16)

                @pl.when(seq + 2 * step < NSEQ)
                def _():
                    copy(r + 1, h).start()

            @pl.when(seq >= step)
            def _():
                if r == 0:
                    before[h] = arrived[r, h].astype(F32)
                else:
                    top, low = compose(arrived[r, h], before[h])
                    before[h, 0:DH] = top
                    before[h, DH:] = low

    for h in range(NH):
        state_ref[h] = before[h, DH:]
    for r in range(ROUNDS):
        @pl.when(seq + 2**r < NSEQ)
        def _():
            for h in range(NH):
                copy(r, h).wait_send()


def scan_states(maps):
    return pl.pallas_call(
        scan_kernel,
        out_shape=jax.ShapeDtypeStruct((NH, DH, DH), F32),
        in_specs=[VMEM],
        out_specs=VMEM,
        scratch_shapes=[
            pltpu.VMEM((ROUNDS, NH, 2 * DH, DH), BF16),
            pltpu.VMEM((ROUNDS, NH, 2 * DH, DH), BF16),
            pltpu.VMEM((NH, 2 * DH, DH), F32),
            pltpu.VMEM((NH, 2 * DH, DH), F32),
            DMA((ROUNDS, NH)),
            DMA((ROUNDS, NH)),
        ],
        compiler_params=pltpu.CompilerParams(
            collective_id=1, has_side_effects=True, vmem_limit_bytes=24 << 20
        ),
        name="scan_states",
    )(maps)


def output_kernel(core_ref, qt_ref, gate_ref, state_ref, gain_ref, wout_ref, out_ref, gated):
    gain = gain_ref[...].reshape(1, DH)
    for h in range(NH):
        core = core_ref[h] + nt(qt_ref[h], state_ref[h])
        scale = lax.rsqrt(jnp.mean(core * core, axis=-1, keepdims=True) + 1e-6)
        z = gate_ref[:, pl.ds(h * DH, DH)].astype(F32)
        gated[:, pl.ds(h * DH, DH)] = (core * scale * gain * silu(z)).astype(BF16)
    for j in range(D // 256):
        out_ref[:, pl.ds(j * 256, 256)] = jnp.dot(
            gated[...], wout_ref[:, pl.ds(j * 256, 256)], preferred_element_type=F32
        ).astype(BF16)


def output_terms(core, qt, gate, states, norm_gain, w_out):
    return pl.pallas_call(
        output_kernel,
        out_shape=jax.ShapeDtypeStruct((BLK, D), BF16),
        in_specs=[VMEM] * 6,
        out_specs=VMEM,
        scratch_shapes=[pltpu.VMEM((BLK, GV), BF16)],
        compiler_params=pltpu.CompilerParams(vmem_limit_bytes=40 << 20),
        name="output_terms",
    )(core, qt, gate, states, norm_gain, w_out)


def scatter_kernel(term_ref, out_ref, arrived, send, recv):
    seq, fsdp, _, zhi, core = coords()
    peers = [zhi * 2 + 1 - core, (1 - zhi) * 2 + core, (1 - zhi) * 2 + 1 - core]
    barrier = pltpu.get_barrier_semaphore()
    for peer in peers:
        pl.semaphore_signal(barrier, inc=1, device_id=(seq, peer), device_id_type=MESH)
    pl.semaphore_wait(barrier, 3)
    copies = []
    for i, peer in enumerate(peers):
        copy = pltpu.make_async_remote_copy(
            term_ref.at[pl.ds(pl.multiple_of(peer * TOK, TOK), TOK)],
            arrived.at[i], send.at[i], recv.at[i],
            device_id=(seq, peer), device_id_type=MESH,
        )
        copy.start()
        copies.append(copy)
    for copy in copies:
        copy.wait()
    total = term_ref[pl.ds(pl.multiple_of(fsdp * TOK, TOK), TOK), :].astype(F32)
    for i in range(3):
        total = total + arrived[i].astype(F32)
    out_ref[...] = total.astype(BF16)


def scatter(terms):
    return pl.pallas_call(
        scatter_kernel,
        out_shape=jax.ShapeDtypeStruct((TOK, D), BF16),
        in_specs=[VMEM],
        out_specs=VMEM,
        scratch_shapes=[pltpu.VMEM((3, TOK, D), BF16), DMA((3,)), DMA((3,))],
        compiler_params=pltpu.CompilerParams(
            collective_id=2, has_side_effects=True, vmem_limit_bytes=24 << 20
        ),
        name="scatter",
    )(terms)


def shards(
    tokens, w_query, w_key, w_value, w_gate_out, w_beta, w_decay,
    conv_weight, decay_log, dt_bias, norm_gain, w_out,
):
    wba = jnp.concatenate([w_beta, w_decay], axis=1).T
    tok_all, w_all, wba_all = gather(tokens, w_query, w_key, w_value, w_gate_out, wba)
    core, qt, gate, maps = local_terms(tok_all, w_all, wba_all, conv_weight, decay_log, dt_bias)
    states = scan_states(maps)
    terms = output_terms(core, qt, gate, states, norm_gain, w_out)
    return scatter(terms)


def solution(mesh):
    return jax.shard_map(
        shards,
        mesh=mesh,
        in_specs=(
            P(("seq", "fsdp"), None),
            P("fsdp", None), P("fsdp", None), P("fsdp", None), P("fsdp", None),
            P("fsdp", None), P("fsdp", None),
            P(), P(), P(), P(),
            P("fsdp", None),
        ),
        out_specs=P(("seq", "fsdp"), None),
        check_vma=False,
    )
```

```python
import functools

import jax
import jax.numpy as jnp
from jax import lax
from jax.experimental import pallas as pl
from jax.experimental.pallas import tpu as pltpu
from jax.sharding import PartitionSpec as P

MESH = pl.DeviceIdType.MESH
F32 = jnp.float32
BF16 = jnp.bfloat16
HBM = pl.BlockSpec(memory_space=pltpu.HBM)
VMEM = pl.BlockSpec(memory_space=pltpu.VMEM)
SMEM = pl.BlockSpec(memory_space=pltpu.SMEM)
DMA = pltpu.SemaphoreType.DMA

D = 2048
DSH = 512
TOK = 128
BLK = 512
HALO = 16
ROWS = HALO + BLK
GQ, GV = 256, 512
GC = 2 * GQ + 2 * GV
DH = 128
NH = 4
NCH = BLK // DH
NSEQ = 32
ROUNDS = 5


def coords():
    seq, fsdp = lax.axis_index("seq"), lax.axis_index("fsdp")
    return seq, fsdp, seq % 2, fsdp // 2, fsdp % 2


def nn(a, b):
    return jnp.dot(a.astype(BF16), b.astype(BF16), preferred_element_type=F32)


def full(a, b):
    return jnp.dot(a, b, preferred_element_type=F32, precision=lax.Precision.HIGHEST)


def split(a):
    high = a.astype(BF16)
    return high, (a - high.astype(F32)).astype(BF16)


def silu(v):
    return v / (1.0 + jnp.exp(-v))


SECTIONS = ((0, GQ), (GQ, GQ), (2 * GQ, GV), (2 * GQ + GV, GV))
PIECE = DSH // 4
UNITS = NCH * NH
TOGETHER = 8


def layer_kernel(
    tok_ref, wq_ref, wk_ref, wv_ref, wz_ref, wba_ref, wo_ref, conv_ref, rate_ref, bias_ref, gain_ref,
    out_ref,
    tok_all, w_all, wba_all, mixed, act, small, cols, key_t, system, scores,
    core_ref, qt_ref, gate_ref, wo_all, outgoing, arrived, window, before, gated, gated_all, total_ref,
    tok_send, tok_recv, ba_send, ba_recv, near_send, near_recv, cut_send, cut_recv,
    ring_send, ring_recv, loc, wo_send, wo_recv, scan_send, scan_recv, gate_send, gate_recv,
):
    seq, fsdp, zlo, zhi, core = coords()
    x, y = seq // 8, (seq // 2) % 4
    sibling = (seq, zhi * 2 + 1 - core)
    far = (1 - zhi) * 2
    across = (seq, far + core)
    cross = (seq, far + 1 - core)
    partner = seq - zlo + 1 - zlo
    partners = [(partner, far + core), (partner, far + 1 - core)]
    rings = [
        [(lax.rem(x + d, 4) * 8 + y * 2 + zlo, fsdp) for d in (1, 3, 2)],
        [(x * 8 + lax.rem(y + d, 4) * 2 + zlo, fsdp) for d in (1, 3, 2)],
    ]
    sends_halo = jnp.logical_and(fsdp == 3, seq < NSEQ - 1)

    barrier = pltpu.get_barrier_semaphore()
    for peer in [sibling, across, cross] + partners + rings[0] + rings[1]:
        pl.semaphore_signal(barrier, inc=1, device_id=peer, device_id_type=MESH)
    for r in range(ROUNDS):
        @pl.when(seq >= 2**r)
        def _():
            pl.semaphore_signal(
                barrier, inc=1, device_id=(seq - 2**r, fsdp), device_id_type=MESH
            )

    @pl.when(seq > 0)
    def _():
        pl.semaphore_signal(barrier, inc=1, device_id=(seq - 1, 3), device_id_type=MESH)

    def remote(source, target, send, recv, peer):
        return pltpu.make_async_remote_copy(
            source, target, send, recv, device_id=peer, device_id_type=MESH
        )

    def token_rows(group):
        return tok_all.at[pl.ds(pl.multiple_of(HALO + group * TOK, 16), TOK)]

    weights = (wq_ref, wk_ref, wv_ref, wz_ref)

    def columns(section, group):
        width = SECTIONS[section][1]
        return pl.ds(pl.multiple_of(group * width, width), width)

    def held(shard, rows, section):
        start, width = SECTIONS[section]
        return w_all.at[shard, rows, pl.ds(start, width)]

    all_rows = pl.ds(0, DSH)
    local = [(tok_ref, token_rows(fsdp)), (wba_ref, wba_all.at[fsdp])] + [
        (weights[section].at[:, columns(section, fsdp)], held(fsdp, all_rows, section))
        for section in range(4)
    ] + [(wo_ref, wo_all.at[fsdp])]
    local_copies = [
        pltpu.make_async_copy(source, target, loc.at[i])
        for i, (source, target) in enumerate(local)
    ]
    for copy in local_copies:
        copy.start()

    onward = sum((seq + 2**r < NSEQ).astype(jnp.int32) for r in range(ROUNDS))
    pl.semaphore_wait(barrier, 11 + 4 * sends_halo.astype(jnp.int32) + onward)

    tok_copies = [
        remote(tok_ref, token_rows(fsdp), tok_send.at[i], tok_recv.at[i], peer)
        for i, peer in enumerate((across, sibling))
    ]
    for copy in tok_copies:
        copy.start()

    piece_at = jnp.where(core == 0, x, y)
    own_piece = pl.ds(pl.multiple_of(piece_at * PIECE, PIECE), PIECE)

    def cut_copy(section, i):
        peer = partners[i]
        return remote(
            weights[section].at[own_piece, columns(section, peer[1])],
            held(fsdp, own_piece, section),
            cut_send.at[i, section], cut_recv.at[core, section], peer,
        )

    for section in range(4):
        for i in range(2):
            cut_copy(section, i).start()

    def halo_copy(k):
        return remote(
            tok_ref.at[pl.ds(TOK - HALO, HALO)], tok_all.at[pl.ds(0, HALO)],
            tok_send.at[3 + k], tok_recv.at[3], (lax.rem(seq + 1, NSEQ), k),
        )

    @pl.when(sends_halo)
    def _():
        for k in range(4):
            halo_copy(k).start()

    ba_copies = [
        remote(wba_ref, wba_all.at[fsdp], ba_send.at[i], ba_recv.at[i], peer)
        for i, peer in enumerate([sibling] + partners)
    ]
    for copy in ba_copies:
        copy.start()

    near_copies = [
        remote(
            weights[section].at[:, columns(section, sibling[1])],
            held(fsdp, all_rows, section),
            near_send.at[section], near_recv.at[section], sibling,
        )
        for section in range(4)
    ]
    for copy in near_copies:
        copy.start()

    places = [x, y]

    def ring_copy(section, shard, i):
        rows = pl.ds(pl.multiple_of(places[shard] * PIECE, PIECE), PIECE)
        block = held(far + shard, rows, section)
        return remote(
            block, block, ring_send.at[shard, i, section], ring_recv.at[shard, i, section],
            rings[shard][i],
        )

    def pass_round(section):
        for shard in range(2):
            rows = pl.ds(pl.multiple_of(places[shard] * PIECE, PIECE), PIECE)
            block = held(far + shard, rows, section)
            remote(
                block, block, cut_send.at[0, section], cut_recv.at[shard, section], partners[0]
            ).wait_recv()
            for i in range(3):
                ring_copy(section, shard, i).start()

    wo_at = pl.ds(pl.multiple_of(piece_at * PIECE, PIECE), PIECE)
    wo_ring = [
        (jnp.where(core == 0, rings[0][i][0], rings[1][i][0]), fsdp) for i in range(3)
    ]

    def wo_beside():
        return remote(wo_ref, wo_all.at[fsdp], wo_send.at[0], wo_recv.at[0], sibling)

    def wo_cut():
        return remote(
            wo_ref.at[wo_at], wo_all.at[fsdp, wo_at], wo_send.at[1], wo_recv.at[1], partners[0]
        )

    def wo_round(i):
        block = wo_all.at[far + core, wo_at]
        return remote(block, block, wo_send.at[2 + i], wo_recv.at[2 + i], wo_ring[i])

    def wo_share():
        block = wo_all.at[far + core]
        return remote(block, block, wo_send.at[5], wo_recv.at[5], sibling)

    def arrive(section):
        local_copies[2 + section].wait()
        near_copies[section].wait_recv()
        for shard in range(2):
            for i in range(3):
                ring_copy(section, shard, i).wait_recv()

    def project(j):
        total = None
        for part in range(4):
            term = jnp.dot(
                tok_all[:, pl.ds(part * DSH, DSH)],
                w_all[part, :, pl.ds(j * 256, 256)],
                preferred_element_type=F32,
            )
            total = term if total is None else total + term
        return total

    def convolve(j):
        mixed[...] = project(j).astype(BF16).astype(F32)

        @pl.when(seq == 0)
        def _():
            mixed[pl.ds(0, HALO), :] = jnp.zeros((HALO, 256), F32)

        if j < 2:
            at = j * 1024 + fsdp * GQ
        else:
            at = 2048 + fsdp * GV + (j - 2) * 256
        taps = conv_ref[:, pl.ds(pl.multiple_of(at, 256), 256)].astype(F32)
        total = taps[0:1, :] * mixed[pl.ds(HALO - 3, BLK), :]
        for i in range(1, 4):
            total = total + taps[i : i + 1, :] * mixed[pl.ds(HALO - 3 + i, BLK), :]
        out = silu(total).astype(BF16).astype(F32)
        for part in range(2):
            head = out[:, part * DH : (part + 1) * DH]
            if j < 2:
                head = head * lax.rsqrt(jnp.sum(head * head, axis=-1, keepdims=True) + 1e-6)
                if j == 0:
                    head = head * DH**-0.5
            act[2 * j + part] = head

    at_row = lax.broadcasted_iota(jnp.int32, (DH, DH), 0)
    at_col = lax.broadcasted_iota(jnp.int32, (DH, DH), 1)
    strict = at_row > at_col
    within = at_row >= at_col
    eye = (at_row == at_col).astype(F32)
    upper = (at_row <= at_col).astype(F32)

    pass_round(0)
    tok_copies[0].wait_recv()
    pass_on = remote(
        token_rows(across[1]), token_rows(across[1]), tok_send.at[2], tok_recv.at[2], sibling
    )
    pass_on.start()
    pass_round(1)

    local_copies[0].wait()
    local_copies[1].wait()
    tok_copies[1].wait_recv()
    pass_on.wait_recv()
    for copy in ba_copies:
        copy.wait_recv()

    @pl.when(seq > 0)
    def _():
        halo_copy(0).wait_recv()

    row = lax.broadcasted_iota(jnp.int32, (8, 32), 0)
    col = lax.broadcasted_iota(jnp.int32, (8, 32), 1)
    pick = (col == jnp.where(row < 4, 0, 12) + fsdp * 4 + row).astype(BF16)
    rows = None
    for part in range(4):
        own = jnp.dot(pick, wba_all[part], preferred_element_type=F32).astype(BF16)
        term = lax.dot_general(
            own, tok_all[pl.ds(HALO, BLK), pl.ds(part * DSH, DSH)],
            (((1,), (1,)), ((), ())), preferred_element_type=F32,
        )
        rows = term if rows is None else rows + term
    rows = rows.astype(BF16).astype(F32)
    beta_rows = jax.nn.sigmoid(rows[0:4])
    which = lax.broadcasted_iota(jnp.int32, (4, 1), 0)
    rate = jnp.zeros((4, 1), F32)
    bias = jnp.zeros((4, 1), F32)
    for h in range(4):
        rate = jnp.where(which == h, rate_ref[fsdp * 4 + h], rate)
        bias = jnp.where(which == h, bias_ref[fsdp * 4 + h], bias)
    decay_rows = -jnp.exp(rate) * jax.nn.softplus(rows[4:8] + bias)
    for n in range(NCH):
        at = slice(n * DH, (n + 1) * DH)
        pair = jnp.concatenate([decay_rows[:, at], beta_rows[:, at]], axis=0)
        cumul = full(pair, upper)
        small[n] = cumul
        cols[n] = jnp.concatenate([cumul[0:4], pair[4:8]], axis=0).T

    arrive(0)
    convolve(0)
    pass_round(2)
    arrive(1)
    convolve(1)
    pass_round(3)

    def fall_of(n, h):
        gap = cols[n][:, h : h + 1] - small[n][h : h + 1, :]
        return jnp.where(within, jnp.exp(jnp.where(within, gap, 0.0)), 0.0)

    def pairs(n, carry):
        tokens = pl.ds(pl.multiple_of(n * DH, DH), DH)
        for kh in range(2):
            q = act[kh, tokens, :]
            k = act[2 + kh, tokens, :]
            kt = k.T.astype(BF16)
            key_t[n * 2 + kh] = kt
            both = nn(jnp.concatenate([k, q], axis=0), kt)
            for h in (2 * kh, 2 * kh + 1):
                fall = fall_of(n, h)
                b = cols[n][:, 4 + h : 5 + h]
                system[n * NH + h] = jnp.where(strict, b * both[:DH] * fall, 0.0).astype(BF16)
                scores[n * NH + h] = (both[DH:] * fall).astype(BF16)
        return carry

    lax.fori_loop(0, NCH, pairs, 0)

    def same(size):
        return at_row // size == at_col // size

    mask8 = jnp.logical_and(strict, same(8)).astype(BF16)
    mask32 = jnp.logical_and(strict, jnp.logical_and(same(32), jnp.logical_not(same(8)))).astype(BF16)
    mask128 = jnp.logical_and(strict, jnp.logical_not(same(32))).astype(BF16)

    def invert(g, carry):
        ids = [g * TOGETHER + i for i in range(TOGETHER)]
        every = range(TOGETHER)
        a1 = [system[u] * mask8 for u in ids]
        a2 = [nn(a, a) for a in a1]
        a34 = [nn(jnp.concatenate([a1[i], a2[i].astype(BF16)], axis=0), a2[i]) for i in every]
        xs = [eye - a1[i].astype(F32) + a2[i] - a34[i][:DH] for i in every]
        xs = [(xs[i] + nn(xs[i], a34[i][DH:])).astype(BF16) for i in every]
        for mask in (mask32, mask128):
            ys = [nn(xs[i], system[ids[i]] * mask).astype(BF16) for i in every]
            yx = [nn(ys[i], jnp.concatenate([ys[i], xs[i]], axis=1)) for i in every]
            zs = [(xs[i].astype(F32) - yx[i][:, DH:]).astype(BF16) for i in every]
            xs = [(zs[i].astype(F32) + nn(yx[i][:, :DH], zs[i])).astype(BF16) for i in every]
        for i in every:
            system[ids[i]] = xs[i]
        return carry

    lax.fori_loop(0, UNITS // TOGETHER, invert, 0)

    arrive(2)
    wo_beside().start()
    wo_cut().start()
    convolve(2)
    convolve(3)

    def scan_copy(r, h):
        cut = pl.ds(0, 2 * DH) if r < ROUNDS - 1 else pl.ds(DH, DH)
        return remote(
            outgoing.at[r, h, :, cut], arrived.at[r, h, :, cut],
            scan_send.at[r, h], scan_recv.at[r, h], (lax.rem(seq + 2**r, NSEQ), fsdp),
        )

    def send_window(r, h):
        outgoing[r, h] = window[h].astype(BF16)

        @pl.when(seq + 2**r < NSEQ)
        def _():
            scan_copy(r, h).start()

    def chunks_of(h):
        every = range(NCH)
        solved, seen, maps = [], [], []
        for n in every:
            at = pl.ds(n * DH, DH)
            k = act[2 + h // 2, at, :]
            c = cols[n][:, h : h + 1]
            b = cols[n][:, 4 + h : 5 + h]
            right = jnp.concatenate([b * act[4 + h, at, :], (b * jnp.exp(c)) * k], axis=1)
            solved.append(nn(system[n * NH + h], right))
        for n in every:
            c = cols[n][:, h : h + 1]
            last = small[n][h : h + 1, DH - 1 : DH]
            maps.append(nn(key_t[n * 2 + h // 2], solved[n] * jnp.exp(last - c)))
            seen.append(nn(scores[n * NH + h], solved[n]))
        so_far = None
        for n in every:
            at = pl.ds(n * DH, DH)
            last = small[n][h : h + 1, DH - 1 : DH]
            transfer = jnp.exp(last) * eye - maps[n][:, DH:]
            query_eff = jnp.exp(cols[n][:, h : h + 1]) * act[h // 2, at, :] - seen[n][:, DH:]
            if n == 0:
                qt_ref[h, at, :] = query_eff.astype(BF16)
                core_ref[h, at, :] = seen[n][:, :DH]
                so_far = jnp.concatenate([transfer, maps[n][:, :DH]], axis=1)
            else:
                both = nn(query_eff, so_far)
                qt_ref[h, at, :] = both[:, :DH].astype(BF16)
                core_ref[h, at, :] = seen[n][:, :DH] + both[:, DH:]
                after = nn(transfer, so_far)
                so_far = jnp.concatenate(
                    [after[:, :DH], after[:, DH:] + maps[n][:, :DH]], axis=1
                )
        window[h] = so_far
        before[h] = jnp.zeros((DH, 2 * DH), F32)
        send_window(0, h)

    def compose(later, earlier):
        high, low = split(later[:, 0:DH])
        dot = functools.partial(jnp.dot, preferred_element_type=F32)
        return dot(high, earlier) + dot(low, earlier)

    def scan_step(r, h):
        step = 2**r

        @pl.when(seq >= step)
        def _():
            scan_copy(r, h).wait_recv()
            if r < ROUNDS - 1:
                out = compose(window[h], arrived[r, h])
                window[h, :, DH:] = out[:, DH:] + window[h, :, DH:]
                window[h, :, 0:DH] = out[:, :DH]

        if r < ROUNDS - 1:
            send_window(r + 1, h)

        @pl.when(seq >= step)
        def _():
            if r == 0:
                before[h] = arrived[r, h].astype(F32)
            elif r < ROUNDS - 1:
                out = compose(before[h], arrived[r, h])
                before[h, :, DH:] = out[:, DH:] + before[h, :, DH:]
                before[h, :, 0:DH] = out[:, :DH]
            else:
                out = compose(before[h], arrived[r, h, :, DH:])
                before[h, :, DH:] = out + before[h, :, DH:]

    mates = [sibling, across, cross]

    def gate_copy(i, h):
        rows = pl.ds(pl.multiple_of(mates[i][1] * TOK, TOK), TOK)
        return remote(
            gated.at[h, rows], gated_all.at[fsdp * NH + h],
            gate_send.at[i, h], gate_recv.at[i, h], mates[i],
        )

    def finish(h):
        core_rows = core_ref[h] + nn(qt_ref[h], before[h, :, DH:])
        scale = lax.rsqrt(jnp.mean(core_rows * core_rows, axis=-1, keepdims=True) + 1e-6)
        z = gate_ref[:, pl.ds(h * DH, DH)].astype(F32)
        gain = gain_ref[...].reshape(1, DH)
        gated[h] = (core_rows * scale * gain * silu(z)).astype(BF16)
        for i in (1, 2, 0):
            gate_copy(i, h).start()
        gated_all[fsdp * NH + h] = gated[h, pl.ds(pl.multiple_of(fsdp * TOK, TOK), TOK), :]

    for wave in range(NH + ROUNDS - 1):
        if wave < NH:
            chunks_of(wave)
        if wave == 1:
            wo_cut().wait_recv()
            for i in range(3):
                wo_round(i).start()
        if wave == NH:
            arrive(3)
            for j in range(2):
                gate_ref[:, pl.ds(j * 256, 256)] = project(4 + j)[HALO:].astype(BF16)
            for i in range(3):
                wo_round(i).wait_recv()
            wo_share().start()
        for h in range(NH):
            r = wave - 1 - h
            if 0 <= r < ROUNDS:
                scan_step(r, h)
                if r == ROUNDS - 1:
                    finish(h)
    scan_step(ROUNDS - 1, NH - 1)
    finish(NH - 1)

    def terms(groups, first):
        for j in range(D // 512):
            at = pl.ds(j * 512, 512)
            total = None if first else total_ref[:, at]
            for group in groups:
                held_rows = jnp.concatenate(
                    [gated_all[group * NH + h] for h in range(NH)], axis=1
                )
                term = jnp.dot(held_rows, wo_all[group, :, at], preferred_element_type=F32)
                total = term if total is None else total + term
            if first:
                total_ref[:, at] = total
            else:
                out_ref[:, at] = total.astype(BF16)

    local_copies[6].wait()
    wo_beside().wait_recv()
    for h in range(NH):
        gate_copy(0, h).wait_recv()
    terms((fsdp, sibling[1]), True)
    wo_share().wait_recv()
    for h in range(NH):
        for i in (1, 2):
            gate_copy(i, h).wait_recv()
    terms((far, far + 1), False)

    tok_copies[0].wait_send()
    tok_copies[1].wait_send()
    pass_on.wait_send()
    for copy in ba_copies + near_copies:
        copy.wait_send()
    for section in range(4):
        for i in range(2):
            cut_copy(section, i).wait_send()
        for shard in range(2):
            for i in range(3):
                ring_copy(section, shard, i).wait_send()

    @pl.when(sends_halo)
    def _():
        for k in range(4):
            halo_copy(k).wait_send()

    wo_beside().wait_send()
    wo_cut().wait_send()
    for i in range(3):
        wo_round(i).wait_send()
    wo_share().wait_send()
    for r in range(ROUNDS):
        @pl.when(seq + 2**r < NSEQ)
        def _():
            for h in range(NH):
                scan_copy(r, h).wait_send()
    for h in range(NH):
        for i in range(3):
            gate_copy(i, h).wait_send()


def layer(
    tokens, w_query, w_key, w_value, w_gate, wba, w_out, conv_weight, decay_log, dt_bias, norm_gain
):
    return pl.pallas_call(
        layer_kernel,
        out_shape=jax.ShapeDtypeStruct((TOK, D), BF16),
        in_specs=[HBM] * 5 + [VMEM, HBM, VMEM, SMEM, SMEM, VMEM],
        out_specs=VMEM,
        scratch_shapes=[
            pltpu.VMEM((ROWS, D), BF16),
            pltpu.VMEM((4, DSH, GC), BF16),
            pltpu.VMEM((4, 32, DSH), BF16),
            pltpu.VMEM((ROWS, 256), F32),
            pltpu.VMEM((8, BLK, DH), F32),
            pltpu.VMEM((NCH, 8, DH), F32),
            pltpu.VMEM((NCH, DH, 8), F32),
            pltpu.VMEM((NCH * 2, DH, DH), BF16),
            pltpu.VMEM((UNITS, DH, DH), BF16),
            pltpu.VMEM((UNITS, DH, DH), BF16),
            pltpu.VMEM((NH, BLK, DH), F32),
            pltpu.VMEM((NH, BLK, DH), BF16),
            pltpu.VMEM((BLK, GV), BF16),
            pltpu.VMEM((4, DSH, D), BF16),
            pltpu.VMEM((ROUNDS, NH, DH, 2 * DH), BF16),
            pltpu.VMEM((ROUNDS, NH, DH, 2 * DH), BF16),
            pltpu.VMEM((NH, DH, 2 * DH), F32),
            pltpu.VMEM((NH, DH, 2 * DH), F32),
            pltpu.VMEM((NH, BLK, DH), BF16),
            pltpu.VMEM((4 * NH, TOK, DH), BF16),
            pltpu.VMEM((TOK, D), F32),
            DMA((7,)), DMA((4,)), DMA((3,)), DMA((3,)), DMA((4,)), DMA((4,)),
            DMA((2, 4)), DMA((2, 4)), DMA((2, 3, 4)), DMA((2, 3, 4)), DMA((7,)),
            DMA((6,)), DMA((6,)), DMA((ROUNDS, NH)), DMA((ROUNDS, NH)), DMA((3, NH)), DMA((3, NH)),
        ],
        compiler_params=pltpu.CompilerParams(
            collective_id=0, has_side_effects=True, vmem_limit_bytes=54 << 20
        ),
        name="layer",
    )(
        tokens, w_query, w_key, w_value, w_gate, wba, w_out, conv_weight, decay_log, dt_bias, norm_gain
    )


def shards(
    tokens, w_query, w_key, w_value, w_gate_out, w_beta, w_decay,
    conv_weight, decay_log, dt_bias, norm_gain, w_out,
):
    wba = jnp.concatenate([w_beta, w_decay], axis=1).T
    return layer(
        tokens, w_query, w_key, w_value, w_gate_out, wba, w_out,
        conv_weight, decay_log, dt_bias, norm_gain,
    )


def solution(mesh):
    return jax.shard_map(
        shards,
        mesh=mesh,
        in_specs=(
            P(("seq", "fsdp"), None),
            P("fsdp", None), P("fsdp", None), P("fsdp", None), P("fsdp", None),
            P("fsdp", None), P("fsdp", None),
            P(), P(), P(), P(),
            P("fsdp", None),
        ),
        out_specs=P(("seq", "fsdp"), None),
        check_vma=False,
    )
```

```python
import functools

import jax
import jax.numpy as jnp
from jax import lax
from jax.experimental import pallas as pl
from jax.experimental.pallas import tpu as pltpu
from jax.sharding import PartitionSpec as P

MESH = pl.DeviceIdType.MESH
F32 = jnp.float32
BF16 = jnp.bfloat16
HBM = pl.BlockSpec(memory_space=pltpu.HBM)
VMEM = pl.BlockSpec(memory_space=pltpu.VMEM)
SMEM = pl.BlockSpec(memory_space=pltpu.SMEM)
DMA = pltpu.SemaphoreType.DMA

D = 2048
DSH = 512
TOK = 128
BLK = 512
HALO = 16
ROWS = HALO + BLK
GQ, GV = 256, 512
GC = 2 * GQ + 2 * GV
DH = 128
NH = 4
NCH = BLK // DH
NSEQ = 32
ROUNDS = 5


def coords():
    seq, fsdp = lax.axis_index("seq"), lax.axis_index("fsdp")
    return seq, fsdp, seq % 2, fsdp // 2, fsdp % 2


def nn(a, b):
    return jnp.dot(a.astype(BF16), b.astype(BF16), preferred_element_type=F32)


def full(a, b):
    return jnp.dot(a, b, preferred_element_type=F32, precision=lax.Precision.HIGHEST)


def split(a):
    high = a.astype(BF16)
    return high, (a - high.astype(F32)).astype(BF16)


def silu(v):
    return v / (1.0 + jnp.exp(-v))


SECTIONS = ((0, GQ), (GQ, GQ), (2 * GQ, GV), (2 * GQ + GV, GV))
PIECE = DSH // 4
HALF = PIECE // 2
STAGES = ((0, 2 * GQ, (0, 1)), (2 * GQ, GV, (2,)), (2 * GQ + GV, GV, (3,)))
UNITS = NCH * NH
TOGETHER = 8


def layer_kernel(
    tok_ref, wq_ref, wk_ref, wv_ref, wz_ref, wba_ref, wo_ref, conv_ref, rate_ref, bias_ref, gain_ref,
    out_ref,
    tok_all, w_all, wba_all, mixed, act, small, cols, key_t, system, scores,
    core_ref, qt_ref, gate_ref, wo_all, outgoing, arrived, window, before, gated, gated_far, total_ref,
    sums_out, sums_in,
    tok_send, tok_recv, ba_send, ba_recv, near_send, near_recv, cut_send, cut_recv,
    pair_send, pair_recv, ring_send, ring_recv, loc, wo_send, wo_recv, scan_send, scan_recv, gate_send, gate_recv,
    sum_send, sum_recv,
):
    seq, fsdp, zlo, zhi, core = coords()
    x, y = seq // 8, (seq // 2) % 4
    sibling = (seq, zhi * 2 + 1 - core)
    far = (1 - zhi) * 2
    across = (seq, far + core)
    partner = seq - zlo + 1 - zlo
    partners = [(partner, far + core), (partner, far + 1 - core)]
    rings = [
        [(lax.rem(x + d, 4) * 8 + y * 2 + zlo, fsdp) for d in (1, 3, 2)],
        [(x * 8 + lax.rem(y + d, 4) * 2 + zlo, fsdp) for d in (1, 3, 2)],
    ]
    sends_halo = jnp.logical_and(fsdp == 3, seq < NSEQ - 1)

    twin = (seq - zlo + 1 - zlo, fsdp)
    barrier = pltpu.get_barrier_semaphore()
    for peer in [sibling, across, twin] + partners + rings[0] + rings[1]:
        pl.semaphore_signal(barrier, inc=1, device_id=peer, device_id_type=MESH)
    for r in range(ROUNDS):
        @pl.when(seq >= 2**r)
        def _():
            pl.semaphore_signal(
                barrier, inc=1, device_id=(seq - 2**r, fsdp), device_id_type=MESH
            )

    @pl.when(seq > 0)
    def _():
        pl.semaphore_signal(barrier, inc=1, device_id=(seq - 1, 3), device_id_type=MESH)

    def remote(source, target, send, recv, peer):
        return pltpu.make_async_remote_copy(
            source, target, send, recv, device_id=peer, device_id_type=MESH
        )

    def token_rows(group):
        return tok_all.at[pl.ds(pl.multiple_of(HALO + group * TOK, 16), TOK)]

    weights = (wq_ref, wk_ref, wv_ref, wz_ref)

    def columns(section, group):
        width = SECTIONS[section][1]
        return pl.ds(pl.multiple_of(group * width, width), width)

    def held(shard, rows, section):
        start, width = SECTIONS[section]
        return w_all.at[shard, rows, pl.ds(start, width)]

    all_rows = pl.ds(0, DSH)
    local = [(tok_ref, token_rows(fsdp)), (wba_ref, wba_all.at[fsdp])] + [
        (weights[section].at[:, columns(section, fsdp)], held(fsdp, all_rows, section))
        for section in range(4)
    ] + [(wo_ref, wo_all.at[0])]
    local_copies = [
        pltpu.make_async_copy(source, target, loc.at[i])
        for i, (source, target) in enumerate(local)
    ]
    for copy in local_copies:
        copy.start()

    onward = sum((seq + 2**r < NSEQ).astype(jnp.int32) for r in range(ROUNDS))
    pl.semaphore_wait(barrier, 11 + 4 * sends_halo.astype(jnp.int32) + onward)

    tok_copies = [
        remote(tok_ref, token_rows(fsdp), tok_send.at[i], tok_recv.at[i], peer)
        for i, peer in enumerate((across, sibling))
    ]
    for copy in tok_copies:
        copy.start()

    def halo_copy(k):
        return remote(
            tok_ref.at[pl.ds(TOK - HALO, HALO)], tok_all.at[pl.ds(0, HALO)],
            tok_send.at[3 + k], tok_recv.at[3], (lax.rem(seq + 1, NSEQ), k),
        )

    ba_copies = [
        remote(wba_ref, wba_all.at[fsdp], ba_send.at[i], ba_recv.at[i], peer)
        for i, peer in enumerate([sibling] + partners)
    ]

    piece_at = jnp.where(core == 0, x, y)
    places = [x, y]

    def half_rows(place, half):
        return pl.ds(pl.multiple_of(place * PIECE + half * HALF, HALF), HALF)

    def cut_copy(section, i):
        peer = partners[i]
        rows = half_rows(piece_at, 1 - zlo)
        return remote(
            weights[section].at[rows, columns(section, peer[1])],
            held(fsdp, rows, section),
            cut_send.at[i, section], cut_recv.at[core, section], peer,
        )

    def near_copy(section):
        return remote(
            weights[section].at[:, columns(section, sibling[1])],
            held(fsdp, all_rows, section),
            near_send.at[section], near_recv.at[section], sibling,
        )

    def start_stage(stage):
        for section in STAGES[stage][2]:
            for i in range(2):
                cut_copy(section, i).start()
            near_copy(section).start()

    def block_of(stage, shard, half):
        start, width, _ = STAGES[stage]
        return w_all.at[far + shard, half_rows(places[shard], half), pl.ds(start, width)]

    def pair_copy(stage, shard):
        block = block_of(stage, shard, zlo)
        return remote(
            block, block, pair_send.at[shard, stage], pair_recv.at[shard, stage], twin
        )

    def ring_copy(stage, shard, which, i):
        block = block_of(stage, shard, zlo if which == 0 else 1 - zlo)
        return remote(
            block, block, ring_send.at[stage, which, shard, i],
            ring_recv.at[stage, which, shard, i], rings[shard][i],
        )

    def pass_cut(stage):
        for shard in range(2):
            for section in STAGES[stage][2]:
                block = held(far + shard, half_rows(places[shard], zlo), section)
                remote(
                    block, block, cut_send.at[0, section], cut_recv.at[shard, section],
                    partners[0],
                ).wait_recv()
            pair_copy(stage, shard).start()
            for i in range(3):
                ring_copy(stage, shard, 0, i).start()

    def pass_pair(stage):
        for shard in range(2):
            pair_copy(stage, shard).wait_recv()
            for i in range(3):
                ring_copy(stage, shard, 1, i).start()

    def arrive(stage):
        for section in STAGES[stage][2]:
            local_copies[2 + section].wait()
            near_copy(section).wait_recv()
        for which in range(2):
            for shard in range(2):
                for i in range(3):
                    ring_copy(stage, shard, which, i).wait_recv()

    wo_at = pl.ds(pl.multiple_of(piece_at * PIECE, PIECE), PIECE)
    wo_ring = [
        (jnp.where(core == 0, rings[0][i][0], rings[1][i][0]), fsdp) for i in range(3)
    ]

    def wo_cut():
        return remote(
            wo_ref.at[wo_at], wo_all.at[1, wo_at], wo_send.at[0], wo_recv.at[0], partners[0]
        )

    def wo_round(i):
        block = wo_all.at[1, wo_at]
        return remote(block, block, wo_send.at[1 + i], wo_recv.at[1 + i], wo_ring[i])

    start_stage(0)

    @pl.when(sends_halo)
    def _():
        for k in range(4):
            halo_copy(k).start()

    for copy in ba_copies:
        copy.start()
    start_stage(1)

    def project(j):
        total = None
        for part in range(4):
            term = jnp.dot(
                tok_all[:, pl.ds(part * DSH, DSH)],
                w_all[part, :, pl.ds(j * 256, 256)],
                preferred_element_type=F32,
            )
            total = term if total is None else total + term
        return total

    def convolve(j):
        mixed[...] = project(j).astype(BF16).astype(F32)

        @pl.when(seq == 0)
        def _():
            mixed[pl.ds(0, HALO), :] = jnp.zeros((HALO, 256), F32)

        if j < 2:
            at = j * 1024 + fsdp * GQ
        else:
            at = 2048 + fsdp * GV + (j - 2) * 256
        taps = conv_ref[:, pl.ds(pl.multiple_of(at, 256), 256)].astype(F32)
        total = taps[0:1, :] * mixed[pl.ds(HALO - 3, BLK), :]
        for i in range(1, 4):
            total = total + taps[i : i + 1, :] * mixed[pl.ds(HALO - 3 + i, BLK), :]
        out = silu(total).astype(BF16).astype(F32)
        for part in range(2):
            head = out[:, part * DH : (part + 1) * DH]
            if j < 2:
                head = head * lax.rsqrt(jnp.sum(head * head, axis=-1, keepdims=True) + 1e-6)
                if j == 0:
                    head = head * DH**-0.5
            act[2 * j + part] = head

    at_row = lax.broadcasted_iota(jnp.int32, (DH, DH), 0)
    at_col = lax.broadcasted_iota(jnp.int32, (DH, DH), 1)
    strict = at_row > at_col
    within = at_row >= at_col
    eye = (at_row == at_col).astype(F32)
    upper = (at_row <= at_col).astype(F32)

    pass_cut(0)
    pass_pair(0)
    tok_copies[0].wait_recv()
    pass_on = remote(
        token_rows(across[1]), token_rows(across[1]), tok_send.at[2], tok_recv.at[2], sibling
    )
    pass_on.start()
    pass_cut(1)
    start_stage(2)
    pass_pair(1)

    local_copies[0].wait()
    local_copies[1].wait()
    tok_copies[1].wait_recv()
    pass_on.wait_recv()
    for copy in ba_copies:
        copy.wait_recv()

    @pl.when(seq > 0)
    def _():
        halo_copy(0).wait_recv()

    row = lax.broadcasted_iota(jnp.int32, (8, 32), 0)
    col = lax.broadcasted_iota(jnp.int32, (8, 32), 1)
    pick = (col == jnp.where(row < 4, 0, 12) + fsdp * 4 + row).astype(BF16)
    rows = None
    for part in range(4):
        own = jnp.dot(pick, wba_all[part], preferred_element_type=F32).astype(BF16)
        term = lax.dot_general(
            own, tok_all[pl.ds(HALO, BLK), pl.ds(part * DSH, DSH)],
            (((1,), (1,)), ((), ())), preferred_element_type=F32,
        )
        rows = term if rows is None else rows + term
    rows = rows.astype(BF16).astype(F32)
    beta_rows = jax.nn.sigmoid(rows[0:4])
    which = lax.broadcasted_iota(jnp.int32, (4, 1), 0)
    rate = jnp.zeros((4, 1), F32)
    bias = jnp.zeros((4, 1), F32)
    for h in range(4):
        rate = jnp.where(which == h, rate_ref[fsdp * 4 + h], rate)
        bias = jnp.where(which == h, bias_ref[fsdp * 4 + h], bias)
    decay_rows = -jnp.exp(rate) * jax.nn.softplus(rows[4:8] + bias)
    for n in range(NCH):
        at = slice(n * DH, (n + 1) * DH)
        pair = jnp.concatenate([decay_rows[:, at], beta_rows[:, at]], axis=0)
        cumul = full(pair, upper)
        small[n] = cumul
        cols[n] = jnp.concatenate([cumul[0:4], pair[4:8]], axis=0).T

    arrive(0)
    convolve(0)
    convolve(1)

    def fall_of(n, h):
        gap = cols[n][:, h : h + 1] - small[n][h : h + 1, :]
        return jnp.where(within, jnp.exp(jnp.where(within, gap, 0.0)), 0.0)

    def pairs(n, carry):
        tokens = pl.ds(pl.multiple_of(n * DH, DH), DH)
        for kh in range(2):
            q = act[kh, tokens, :]
            k = act[2 + kh, tokens, :]
            kt = k.T.astype(BF16)
            key_t[n * 2 + kh] = kt
            both = nn(jnp.concatenate([k, q], axis=0), kt)
            for h in (2 * kh, 2 * kh + 1):
                fall = fall_of(n, h)
                b = cols[n][:, 4 + h : 5 + h]
                system[n * NH + h] = jnp.where(strict, b * both[:DH] * fall, 0.0).astype(BF16)
                scores[n * NH + h] = (both[DH:] * fall).astype(BF16)
        return carry

    lax.fori_loop(0, NCH, pairs, 0)
    pass_cut(2)

    def same(size):
        return at_row // size == at_col // size

    mask8 = jnp.logical_and(strict, same(8)).astype(BF16)
    mask32 = jnp.logical_and(strict, jnp.logical_and(same(32), jnp.logical_not(same(8)))).astype(BF16)
    mask128 = jnp.logical_and(strict, jnp.logical_not(same(32))).astype(BF16)

    def invert(g, carry):
        ids = [g * TOGETHER + i for i in range(TOGETHER)]
        every = range(TOGETHER)
        a1 = [system[u] * mask8 for u in ids]
        a2 = [nn(a, a) for a in a1]
        a34 = [nn(jnp.concatenate([a1[i], a2[i].astype(BF16)], axis=0), a2[i]) for i in every]
        xs = [eye - a1[i].astype(F32) + a2[i] - a34[i][:DH] for i in every]
        xs = [(xs[i] + nn(xs[i], a34[i][DH:])).astype(BF16) for i in every]
        for mask in (mask32, mask128):
            ys = [nn(xs[i], system[ids[i]] * mask).astype(BF16) for i in every]
            yx = [nn(ys[i], jnp.concatenate([ys[i], xs[i]], axis=1)) for i in every]
            zs = [(xs[i].astype(F32) - yx[i][:, DH:]).astype(BF16) for i in every]
            xs = [(zs[i].astype(F32) + nn(yx[i][:, :DH], zs[i])).astype(BF16) for i in every]
        for i in every:
            system[ids[i]] = xs[i]
        return carry

    lax.fori_loop(0, UNITS // TOGETHER, invert, 0)

    pass_pair(2)
    wo_cut().start()
    arrive(1)
    convolve(2)
    convolve(3)

    def scan_copy(r, h, part):
        cut = pl.ds(part * DH, DH)
        return remote(
            outgoing.at[r, h, :, cut], arrived.at[r, h, :, cut],
            scan_send.at[r, h, part], scan_recv.at[r, h, part],
            (lax.rem(seq + 2**r, NSEQ), fsdp),
        )

    def parts(r):
        return (0, 1) if r < ROUNDS - 1 else (1,)

    def send_part(r, h, part, value):
        outgoing[r, h, :, pl.ds(part * DH, DH)] = value.astype(BF16)

        @pl.when(seq + 2**r < NSEQ)
        def _():
            scan_copy(r, h, part).start()

    def send_window(r, h):
        for part in parts(r):
            send_part(r, h, part, window[h, :, pl.ds(part * DH, DH)])

    def chunks_of(h):
        every = range(NCH)
        solved, seen, maps = [], [], []
        for n in every:
            at = pl.ds(n * DH, DH)
            k = act[2 + h // 2, at, :]
            c = cols[n][:, h : h + 1]
            b = cols[n][:, 4 + h : 5 + h]
            right = jnp.concatenate([b * act[4 + h, at, :], (b * jnp.exp(c)) * k], axis=1)
            solved.append(nn(system[n * NH + h], right))
        for n in every:
            c = cols[n][:, h : h + 1]
            last = small[n][h : h + 1, DH - 1 : DH]
            maps.append(nn(key_t[n * 2 + h // 2], solved[n] * jnp.exp(last - c)))
            seen.append(nn(scores[n * NH + h], solved[n]))
        so_far = None
        for n in every:
            at = pl.ds(n * DH, DH)
            last = small[n][h : h + 1, DH - 1 : DH]
            transfer = jnp.exp(last) * eye - maps[n][:, DH:]
            query_eff = jnp.exp(cols[n][:, h : h + 1]) * act[h // 2, at, :] - seen[n][:, DH:]
            if n == 0:
                qt_ref[h, at, :] = query_eff.astype(BF16)
                core_ref[h, at, :] = seen[n][:, :DH]
                so_far = jnp.concatenate([transfer, maps[n][:, :DH]], axis=1)
            else:
                both = nn(query_eff, so_far)
                qt_ref[h, at, :] = both[:, :DH].astype(BF16)
                core_ref[h, at, :] = seen[n][:, :DH] + both[:, DH:]
                after = nn(transfer, so_far)
                so_far = jnp.concatenate(
                    [after[:, :DH], after[:, DH:] + maps[n][:, :DH]], axis=1
                )
        window[h] = so_far
        before[h] = jnp.zeros((DH, 2 * DH), F32)
        send_window(0, h)

    def compose(later, earlier):
        high, low = later
        dot = functools.partial(jnp.dot, preferred_element_type=F32)
        return dot(high, earlier) + dot(low, earlier)

    def scan_step(r, h):
        step = 2**r

        @pl.when(seq >= step)
        def _():
            if r < ROUNDS - 1:
                own = split(window[h, :, 0:DH])
                scan_copy(r, h, 0).wait_recv()
                if r < ROUNDS - 2:
                    moved = compose(own, arrived[r, h, :, 0:DH])
                    send_part(r + 1, h, 0, moved)
                    window[h, :, 0:DH] = moved
                scan_copy(r, h, 1).wait_recv()
                shifted = compose(own, arrived[r, h, :, DH:]) + window[h, :, DH:]
                send_part(r + 1, h, 1, shifted)
                window[h, :, DH:] = shifted
                if r == 0:
                    before[h] = arrived[r, h].astype(F32)
                else:
                    out = compose(split(before[h, :, 0:DH]), arrived[r, h])
                    before[h, :, DH:] = out[:, DH:] + before[h, :, DH:]
                    before[h, :, 0:DH] = out[:, :DH]
            else:
                own = split(before[h, :, 0:DH])
                scan_copy(r, h, 1).wait_recv()
                before[h, :, DH:] = compose(own, arrived[r, h, :, DH:]) + before[h, :, DH:]

        if r < ROUNDS - 1:
            @pl.when(seq < step)
            def _():
                send_window(r + 1, h)

    here = pl.ds(pl.multiple_of(zhi * 2 * TOK, TOK), 2 * TOK)
    there = pl.ds(pl.multiple_of(far * TOK, TOK), 2 * TOK)

    def gate_copy(h):
        return remote(
            gated.at[h, there], gated_far.at[h], gate_send.at[h], gate_recv.at[h], across
        )

    def finish(h):
        core_rows = core_ref[h] + nn(qt_ref[h], before[h, :, DH:])
        scale = lax.rsqrt(jnp.mean(core_rows * core_rows, axis=-1, keepdims=True) + 1e-6)
        z = gate_ref[:, pl.ds(h * DH, DH)].astype(F32)
        gain = gain_ref[...].reshape(1, DH)
        gated[h] = (core_rows * scale * gain * silu(z)).astype(BF16)
        gate_copy(h).start()

    for wave in range(NH + ROUNDS - 1):
        if wave < NH:
            chunks_of(wave)
        if wave == 3:
            wo_cut().wait_recv()
            for i in range(3):
                wo_round(i).start()
        if wave == 5:
            arrive(2)
            for j in range(2):
                gate_ref[:, pl.ds(j * 256, 256)] = project(4 + j)[HALO:].astype(BF16)
        for h in range(NH):
            r = wave - 1 - h
            if 0 <= r < ROUNDS:
                scan_step(r, h)
                if r == ROUNDS - 1:
                    finish(h)
    scan_step(ROUNDS - 1, NH - 1)
    finish(NH - 1)

    mine = pl.ds(pl.multiple_of(core * TOK, TOK), TOK)
    others = pl.ds(pl.multiple_of((1 - core) * TOK, TOK), TOK)

    def sum_copy(j):
        at = pl.ds(j * 512, 512)
        return remote(
            sums_out.at[:, at], sums_in.at[:, at], sum_send.at[j], sum_recv.at[j], sibling
        )

    local_copies[6].wait()
    own_rows = jnp.concatenate([gated[h, here, :] for h in range(NH)], axis=1)
    for j in range(D // 512):
        at = pl.ds(j * 512, 512)
        total_ref[:, at] = jnp.dot(own_rows, wo_all[0, :, at], preferred_element_type=F32)
    for i in range(3):
        wo_round(i).wait_recv()
    for h in range(NH):
        gate_copy(h).wait_recv()
    far_rows = jnp.concatenate([gated_far[h] for h in range(NH)], axis=1)
    for j in range(D // 512):
        at = pl.ds(j * 512, 512)
        total_ref[:, at] += jnp.dot(far_rows, wo_all[1, :, at], preferred_element_type=F32)
        sums_out[:, at] = total_ref[others, at].astype(BF16)
        sum_copy(j).start()
    for j in range(D // 512):
        at = pl.ds(j * 512, 512)
        sum_copy(j).wait_recv()
        out_ref[:, at] = (total_ref[mine, at] + sums_in[:, at].astype(F32)).astype(BF16)

    tok_copies[0].wait_send()
    tok_copies[1].wait_send()
    pass_on.wait_send()
    for copy in ba_copies:
        copy.wait_send()
    for section in range(4):
        near_copy(section).wait_send()
        for i in range(2):
            cut_copy(section, i).wait_send()
    for stage in range(3):
        for shard in range(2):
            pair_copy(stage, shard).wait_send()
            for which in range(2):
                for i in range(3):
                    ring_copy(stage, shard, which, i).wait_send()

    @pl.when(sends_halo)
    def _():
        for k in range(4):
            halo_copy(k).wait_send()

    wo_cut().wait_send()
    for i in range(3):
        wo_round(i).wait_send()
    for r in range(ROUNDS):
        @pl.when(seq + 2**r < NSEQ)
        def _():
            for h in range(NH):
                for part in parts(r):
                    scan_copy(r, h, part).wait_send()
    for h in range(NH):
        gate_copy(h).wait_send()
    for j in range(D // 512):
        sum_copy(j).wait_send()


def layer(
    tokens, w_query, w_key, w_value, w_gate, wba, w_out, conv_weight, decay_log, dt_bias, norm_gain
):
    return pl.pallas_call(
        layer_kernel,
        out_shape=jax.ShapeDtypeStruct((TOK, D), BF16),
        in_specs=[HBM] * 5 + [VMEM, HBM, VMEM, SMEM, SMEM, VMEM],
        out_specs=VMEM,
        scratch_shapes=[
            pltpu.VMEM((ROWS, D), BF16),
            pltpu.VMEM((4, DSH, GC), BF16),
            pltpu.VMEM((4, 32, DSH), BF16),
            pltpu.VMEM((ROWS, 256), F32),
            pltpu.VMEM((8, BLK, DH), F32),
            pltpu.VMEM((NCH, 8, DH), F32),
            pltpu.VMEM((NCH, DH, 8), F32),
            pltpu.VMEM((NCH * 2, DH, DH), BF16),
            pltpu.VMEM((UNITS, DH, DH), BF16),
            pltpu.VMEM((UNITS, DH, DH), BF16),
            pltpu.VMEM((NH, BLK, DH), F32),
            pltpu.VMEM((NH, BLK, DH), BF16),
            pltpu.VMEM((BLK, GV), BF16),
            pltpu.VMEM((2, DSH, D), BF16),
            pltpu.VMEM((ROUNDS, NH, DH, 2 * DH), BF16),
            pltpu.VMEM((ROUNDS, NH, DH, 2 * DH), BF16),
            pltpu.VMEM((NH, DH, 2 * DH), F32),
            pltpu.VMEM((NH, DH, 2 * DH), F32),
            pltpu.VMEM((NH, BLK, DH), BF16),
            pltpu.VMEM((NH, 2 * TOK, DH), BF16),
            pltpu.VMEM((2 * TOK, D), F32),
            pltpu.VMEM((TOK, D), BF16),
            pltpu.VMEM((TOK, D), BF16),
            DMA((7,)), DMA((4,)), DMA((3,)), DMA((3,)), DMA((4,)), DMA((4,)),
            DMA((2, 4)), DMA((2, 4)), DMA((2, 3)), DMA((2, 3)),
            DMA((3, 2, 2, 3)), DMA((3, 2, 2, 3)), DMA((7,)),
            DMA((4,)), DMA((4,)), DMA((ROUNDS, NH, 2)), DMA((ROUNDS, NH, 2)), DMA((NH,)), DMA((NH,)),
            DMA((4,)), DMA((4,)),
        ],
        compiler_params=pltpu.CompilerParams(
            collective_id=0, has_side_effects=True, vmem_limit_bytes=54 << 20
        ),
        name="layer",
    )(
        tokens, w_query, w_key, w_value, w_gate, wba, w_out, conv_weight, decay_log, dt_bias, norm_gain
    )


def shards(
    tokens, w_query, w_key, w_value, w_gate_out, w_beta, w_decay,
    conv_weight, decay_log, dt_bias, norm_gain, w_out,
):
    wba = jnp.concatenate([w_beta, w_decay], axis=1).T
    return layer(
        tokens, w_query, w_key, w_value, w_gate_out, wba, w_out,
        conv_weight, decay_log, dt_bias, norm_gain,
    )


def solution(mesh):
    return jax.shard_map(
        shards,
        mesh=mesh,
        in_specs=(
            P(("seq", "fsdp"), None),
            P("fsdp", None), P("fsdp", None), P("fsdp", None), P("fsdp", None),
            P("fsdp", None), P("fsdp", None),
            P(), P(), P(), P(),
            P("fsdp", None),
        ),
        out_specs=P(("seq", "fsdp"), None),
        check_vma=False,
    )
```
